256 devices in a mesh: ha: 8 (over x, y_lo), wa: 32 (over z, y_hi, core).
Axes of the slice: x: 4, y: 4 (y_hi: 2, y_lo: 2; y = y_hi * 2 + y_lo), z: 8, core: 2. Of those that a mesh axis runs over, the one named last changes fastest.
Arguments:
- tokens: bfloat16 [4, 64, 256, 1536], P(None, 'ha', 'wa'), may hold values from -6 to 6
- shift: float32 [1536], replicated, may hold values from -3 to 3
- scale: float32 [1536], replicated, may hold values from -3 to 3
- gate: float32 [1536], replicated, may hold values from -4 to 4
- qkv_weight: bfloat16 [1536, 4608], P('wa'), may hold values from -0.17860863 to 0.17860863
- out_weight: bfloat16 [1536, 1536], P('wa'), may hold values from -0.15625 to 0.15625
- q_gain: float32 [128], replicated, may hold values from 1.4 to 6.5
- k_gain: float32 [128], replicated, may hold values from 1.4 to 6.5
Outputs:
- update: bfloat16 [4, 64, 256, 1536], P(None, 'ha', 'wa')
The draws below stay inside these ranges and needn't reach their ends.
All inputs are finite; a program needn't handle non-finite values.
Results may differ from the reference program's by a relative error of at most 0.009.
The reference program's roundings to bfloat16 on the way count: a program that leaves them out, or rounds other values in their place, can miss the bound.
Values may be sent and summed in bfloat16 or wider, within the bound.
No kernel may reach another device: no remote copies, remote signals or barrier semaphores. Data moves between devices by JAX's collectives and lax.ppermute only.
A program may use at most 128 MiB of HBM per device.

```python
import jax
import jax.numpy as jnp
from jax import lax

D = 1536
HEADS = 12
HD = 128
TILE_T = 4
TILE_H = 8
TILE_W = 8
INNER = 1536
FRAMES = 4
HEIGHT = 64
WIDTH = 256


def draw_tokens(key, part):
    shape = (FRAMES, HEIGHT, WIDTH, D)
    values = jnp.clip(jax.random.normal(key, shape, jnp.float32), -6.0, 6.0)
    return values.astype(jnp.bfloat16)


def draw_qkv_weight(key, part):
    inner = HEADS * HD
    base = jnp.clip(jax.random.normal(key, (D, 3 * inner), jnp.float32), -5.0, 5.0)
    return (base / jnp.sqrt(jnp.float32(D))).astype(jnp.bfloat16)


def draw_gain(key):
    return jax.random.uniform(key, (HD,), jnp.float32, 1.4, 2.6)


def draw_q_gain(key, part):
    return draw_gain(jax.random.fold_in(key, 11))


def draw_k_gain(key, part):
    return draw_gain(jax.random.fold_in(key, 13))


def block_levels(own_key, dims, split, least, largest):
    def one(position, parts):
        steps = jax.random.uniform(jax.random.fold_in(jax.random.fold_in(own_key, 6), position), (parts,), jnp.float32, least / len(split), largest / len(split))
        return jnp.repeat(jnp.exp(steps), dims[position] // parts).reshape((-1,) + (1,) * (len(dims) - position - 1))

    factor_of = one(*split[0])
    for cut in split[1:]:
        factor_of = factor_of * one(*cut)
    return factor_of


def scatter_about(key, shape, width, most, pieces=(), kind=jnp.bfloat16):
    values = width * jax.random.normal(key, shape, jnp.float32)
    if pieces:
        values = values * block_levels(key, shape, pieces, -0.22, 0.18)
    return jnp.clip(values, -most, most).astype(kind)


def setup_inputs(seed: int = 0) -> dict:
    splits = jax.random.split(jax.random.key(seed), 9)
    tokens = draw_tokens(jax.random.fold_in(splits[8], 71), 0)
    shift = scatter_about(splits[1], (D,), 0.5, 3.0, (), jnp.float32)
    scale = scatter_about(splits[2], (D,), 0.5, 3.0, (), jnp.float32)
    gate = scatter_about(splits[3], (D,), 1.0, 4.0, (), jnp.float32)
    qkv_weight = draw_qkv_weight(jax.random.fold_in(splits[8], 71), 0)
    out_weight = scatter_about(splits[5], (INNER, D), INNER ** -0.5, 0.15625, ((0, 32),))
    q_gain = draw_q_gain(jax.random.fold_in(splits[8], 71), 0)
    k_gain = draw_k_gain(jax.random.fold_in(splits[8], 71), 0)
    return dict(tokens=tokens, shift=shift, scale=scale, gate=gate, qkv_weight=qkv_weight, out_weight=out_weight, q_gain=q_gain, k_gain=k_gain)


def reference(tokens, shift, scale, gate, qkv_weight, out_weight, q_gain, k_gain):
    inner = HEADS * HD
    flat = tokens.reshape(-1, D).astype(jnp.float32)
    mean = lax.optimization_barrier(jnp.mean(flat, axis=-1, keepdims=True))
    centred = flat - mean
    var = lax.optimization_barrier(jnp.mean(centred * centred, axis=-1, keepdims=True))
    normed = centred / jnp.sqrt(var + 1e-06)
    modulated = (normed * (1.0 + scale) + shift).astype(jnp.bfloat16)
    projected = jnp.dot(modulated, qkv_weight, preferred_element_type=jnp.float32)
    q_raw = projected[:, :inner].reshape(-1, HEADS, HD)
    k_raw = projected[:, inner:2 * inner].reshape(-1, HEADS, HD)
    query = (q_raw * lax.rsqrt(lax.optimization_barrier(jnp.mean(q_raw * q_raw, axis=-1, keepdims=True)) + 1e-06) * q_gain).astype(jnp.bfloat16)
    key = (k_raw * lax.rsqrt(lax.optimization_barrier(jnp.mean(k_raw * k_raw, axis=-1, keepdims=True)) + 1e-06) * k_gain).astype(jnp.bfloat16)
    value = projected[:, 2 * inner:].astype(jnp.bfloat16)
    query = query.reshape(FRAMES, HEIGHT, WIDTH, HEADS, HD)
    key = key.reshape(FRAMES, HEIGHT, WIDTH, HEADS, HD)
    value = value.reshape(FRAMES, HEIGHT, WIDTH, HEADS, HD)
    pads = ((0, 0), (TILE_H, TILE_H), (TILE_W, TILE_W), (0, 0), (0, 0))
    key_pad = jnp.pad(key, pads)
    value_pad = jnp.pad(value, pads)
    rows_ok = (jnp.arange(HEIGHT + 2 * TILE_H) >= TILE_H) & (jnp.arange(HEIGHT + 2 * TILE_H) < HEIGHT + TILE_H)
    cols_ok = (jnp.arange(WIDTH + 2 * TILE_W) >= TILE_W) & (jnp.arange(WIDTH + 2 * TILE_W) < WIDTH + TILE_W)
    valid_pad = rows_ok[:, None] & cols_ok[None, :]
    tiles_w = WIDTH // TILE_W
    tiles_h = HEIGHT // TILE_H
    groups = FRAMES // TILE_T
    zero = jnp.zeros((), jnp.int32)

    def one_tile(index):
        row0 = (index // tiles_w * TILE_H).astype(jnp.int32)
        col0 = (index % tiles_w * TILE_W).astype(jnp.int32)
        qt = lax.dynamic_slice(query, (zero, row0, col0, zero, zero), (FRAMES, TILE_H, TILE_W, HEADS, HD))
        kt = lax.dynamic_slice(key_pad, (zero, row0, col0, zero, zero), (FRAMES, 3 * TILE_H, 3 * TILE_W, HEADS, HD))
        vt = lax.dynamic_slice(value_pad, (zero, row0, col0, zero, zero), (FRAMES, 3 * TILE_H, 3 * TILE_W, HEADS, HD))
        valid = lax.dynamic_slice(valid_pad, (row0, col0), (3 * TILE_H, 3 * TILE_W))
        valid = jnp.broadcast_to(valid, (TILE_T, 3 * TILE_H, 3 * TILE_W)).reshape(-1)
        qt = qt.reshape(groups, -1, HEADS, HD).astype(jnp.float32)
        kt = kt.reshape(groups, -1, HEADS, HD).astype(jnp.float32)
        vt = vt.reshape(groups, -1, HEADS, HD).astype(jnp.float32)
        scores = jnp.einsum('bqhd,bkhd->bhqk', qt, kt) / jnp.sqrt(jnp.float32(HD))
        scores = jnp.where(valid[None, None, None, :], scores, -jnp.inf)
        top = lax.optimization_barrier(jnp.max(scores, axis=-1, keepdims=True))
        expo = jnp.exp(scores - top)
        total = lax.optimization_barrier(jnp.sum(expo, axis=-1))
        probability_rows = expo.astype(jnp.bfloat16).astype(jnp.float32)
        summed_output = jnp.einsum('bhqk,bkhd->bqhd', probability_rows, vt)
        attended = summed_output / jnp.transpose(total, (0, 2, 1))[..., None]
        return attended.reshape(FRAMES, TILE_H, TILE_W, inner).astype(jnp.bfloat16)
    tiles = lax.map(one_tile, jnp.arange(tiles_h * tiles_w, dtype=jnp.int32))
    tiles = tiles.reshape(tiles_h, tiles_w, FRAMES, TILE_H, TILE_W, inner)
    attended = jnp.transpose(tiles, (2, 0, 3, 1, 4, 5)).reshape(-1, inner)
    output = jnp.dot(attended, out_weight, preferred_element_type=jnp.float32)
    return (gate * output).astype(jnp.bfloat16).reshape(FRAMES, HEIGHT, WIDTH, D)
```

```python
import functools

import jax
import jax.numpy as jnp
from jax import lax
from jax.experimental import pallas as pl
from jax.experimental.pallas import tpu as pltpu
from jax.sharding import Mesh
from jax.sharding import PartitionSpec as P

HEADS = 12
HD = 128
TILE_T = 4
EPS = 1e-06
HALF = 3 * HD
AXES = ("x", "l", "z", "u", "c")
SIZES = (4, 2, 8, 2, 2)
FAR = 1e30
BF = jnp.bfloat16
F32 = jnp.float32


def hops(move):
    pairs = []
    for x in range(4):
        for l in range(2):
            for z in range(8):
                for u in range(2):
                    for c in range(2):
                        h, s = (x * 2 + l, (z * 2 + u) * 2 + c)
                        h2, s2 = move(h, s)
                        pairs.append((h * 32 + s, h2 % 8 * 32 + s2 % 32))
    return pairs


def across(s):
    return s + 1 if s % 2 else s - 1


def flip_y(h, s):
    return (h ^ 1, s ^ 2)


SIBLING = hops(lambda h, s: (h, s ^ 1))
H_UP = hops(lambda h, s: (h + 1, s))
H_DOWN = hops(lambda h, s: (h - 1, s))
SIDE = hops(lambda h, s: (h, across(s)))
SIDE_UP = hops(lambda h, s: (h + 1, across(s)))
SIDE_DOWN = hops(lambda h, s: (h - 1, across(s)))
Y_FLIP = hops(flip_y)
X_UP = hops(lambda h, s: (h + 2, s))
X_DOWN = hops(lambda h, s: (h - 2, s))


def send(x, pairs):
    return lax.ppermute(x, AXES, pairs)


def cost(flops, nbytes, trans=0):
    return pl.CostEstimate(flops=int(flops), bytes_accessed=int(nbytes), transcendentals=int(trans))


def modulate_kernel(x_ref, scale_ref, shift_ref, o_ref):
    x = x_ref[...].astype(F32)
    mean = jnp.mean(x, axis=-1, keepdims=True)
    centred = x - mean
    var = jnp.mean(centred * centred, axis=-1, keepdims=True)
    normed = centred * lax.rsqrt(var + EPS)
    o_ref[...] = (normed * (1.0 + scale_ref[...]) + shift_ref[...]).astype(BF)


def modulate(x, scale, shift):
    rows, width = x.shape
    step = 64
    return pl.pallas_call(
        modulate_kernel,
        out_shape=jax.ShapeDtypeStruct((rows, width), BF),
        grid=(rows // step,),
        in_specs=[
            pl.BlockSpec((step, width), lambda i: (i, 0)),
            pl.BlockSpec((1, width), lambda i: (0, 0)),
            pl.BlockSpec((1, width), lambda i: (0, 0)),
        ],
        out_specs=pl.BlockSpec((step, width), lambda i: (i, 0)),
        cost_estimate=cost(rows * width * 8, rows * width * 4),
        name="modulate",
    )(x, scale.reshape(1, -1), shift.reshape(1, -1))


def head_norm(raw, gain):
    return (raw * lax.rsqrt(jnp.mean(raw * raw, axis=-1, keepdims=True) + EPS) * gain).astype(BF)


def kv_kernel(n, *refs):
    tiles = refs[:n]
    wk_ref, wv_ref, gain_ref, k_ref, v_ref, buf, sem = refs[n:]
    i = pl.program_id(0)

    def fetch(j, slot):
        for t in range(n):

            @pl.when(j == t)
            def _():
                pltpu.make_async_copy(tiles[t], buf.at[slot], sem.at[slot]).start()

    @pl.when(i == 0)
    def _():
        fetch(i, 0)

    slot = lax.rem(i, 2)

    @pl.when(i + 1 < n)
    def _():
        fetch(i + 1, 1 - slot)

    pltpu.make_async_copy(tiles[0], buf.at[slot], sem.at[slot]).wait()
    x = buf[slot]
    raw = jnp.dot(x, wk_ref[...], preferred_element_type=F32)
    for h in range(3):
        k_ref[h] = head_norm(raw[:, h * HD : (h + 1) * HD], gain_ref[...])
    raw = jnp.dot(x, wv_ref[...], preferred_element_type=F32)
    for h in range(3):
        v_ref[h] = raw[:, h * HD : (h + 1) * HD].astype(BF)


def keys_values(tiles, wk, wv, gain):
    n = len(tiles)
    rows, width = tiles[0].shape
    return pl.pallas_call(
        functools.partial(kv_kernel, n),
        out_shape=[jax.ShapeDtypeStruct((3, n * rows, HD), BF)] * 2,
        grid=(n,),
        in_specs=[pl.BlockSpec(memory_space=pl.ANY)] * n
        + [
            pl.BlockSpec((width, HALF), lambda i: (0, 0)),
            pl.BlockSpec((width, HALF), lambda i: (0, 0)),
            pl.BlockSpec((1, HD), lambda i: (0, 0)),
        ],
        out_specs=[pl.BlockSpec((3, rows, HD), lambda i: (0, i, 0))] * 2,
        scratch_shapes=[pltpu.VMEM((2, rows, width), BF), pltpu.SemaphoreType.DMA((2,))],
        compiler_params=pltpu.CompilerParams(vmem_limit_bytes=24 << 20),
        cost_estimate=cost(2 * n * rows * width * 2 * HALF, n * rows * (width + 2 * HALF) * 2),
        name="keys_values",
    )(*tiles, wk, wv, gain)


def query_kernel(x0_ref, x1_ref, w_ref, gain_ref, o_ref):
    for t, x_ref in enumerate((x0_ref, x1_ref)):
        raw = jnp.dot(x_ref[...], w_ref[...], preferred_element_type=F32)
        for h in range(3):
            o_ref[t, h] = head_norm(raw[:, h * HD : (h + 1) * HD], gain_ref[...])


def queries(x0, x1, wq, gain):
    rows, width = x0.shape
    return pl.pallas_call(
        query_kernel,
        out_shape=jax.ShapeDtypeStruct((2, 3, rows, HD), BF),
        in_specs=[pl.BlockSpec(memory_space=pltpu.VMEM)] * 4,
        out_specs=pl.BlockSpec(memory_space=pltpu.VMEM),
        compiler_params=pltpu.CompilerParams(vmem_limit_bytes=16 << 20),
        cost_estimate=cost(4 * rows * width * HALF, rows * (2 * width + 2 * HALF) * 2 + width * HALF * 2),
        name="queries",
    )(x0, x1, wq, gain)


def attend_kernel(far_ref, q_ref, k_ref, v_ref, o_ref):
    tile = pl.program_id(1)
    rows = q_ref.shape[2]
    q = q_ref[0, 0]
    factor = 1.4426950408889634 / jnp.sqrt(F32(HD))
    base = tile * 3
    scores, top = ([], None)
    for j in range(9):
        at = pl.multiple_of((base + j) * rows, rows)
        k = k_ref[0, pl.ds(at, rows), :]
        s = lax.dot_general(q, k, (((1,), (1,)), ((), ())), preferred_element_type=F32)
        scores.append(s)
        most = jnp.max(s, axis=-1, keepdims=True) - far_ref[base + j]
        top = most if top is None else jnp.maximum(top, most)
    total = jnp.zeros((rows, 1), F32)
    acc = jnp.zeros((rows, HD), F32)
    for j in range(9):
        at = pl.multiple_of((base + j) * rows, rows)
        expo = jnp.exp2((scores[j] - (top + far_ref[base + j])) * factor)
        total += jnp.sum(expo, axis=-1, keepdims=True)
        acc += jnp.dot(expo.astype(BF), v_ref[0, pl.ds(at, rows), :], preferred_element_type=F32)
    o_ref[0] = (acc / total).astype(BF)


def attend(far, q, k, v):
    rows = q.shape[2]
    keys = k.shape[1]
    window = 9 * rows
    return pl.pallas_call(
        attend_kernel,
        out_shape=jax.ShapeDtypeStruct((2, rows, HALF), BF),
        grid_spec=pltpu.PrefetchScalarGridSpec(
            num_scalar_prefetch=1,
            grid=(3, 2),
            in_specs=[
                pl.BlockSpec((1, 1, rows, HD), lambda h, t, far: (t, h, 0, 0)),
                pl.BlockSpec((1, keys, HD), lambda h, t, far: (h, 0, 0)),
                pl.BlockSpec((1, keys, HD), lambda h, t, far: (h, 0, 0)),
            ],
            out_specs=pl.BlockSpec((1, rows, HD), lambda h, t, far: (t, 0, h)),
        ),
        compiler_params=pltpu.CompilerParams(vmem_limit_bytes=32 << 20),
        cost_estimate=cost(6 * rows * window * HD * 4, 6 * keys * HD * 2 * 2, 6 * rows * window),
        name="attend",
    )(far, q, k, v)


def project_kernel(at_ref, a0, a1, a2, a3, w0, w1, w2, w3, gate_ref, o_ref, left):
    for j, a in enumerate((a0, a1, a2, a3)):
        left[:, pl.ds(pl.multiple_of(at_ref[j] * HALF, HD), HALF)] = a[...]
    for j, w in enumerate((w0, w1, w2, w3)):
        cols = pl.ds(pl.multiple_of(at_ref[j] * HALF, HD), HALF)
        out = jnp.dot(left[...], w[...], preferred_element_type=F32)
        o_ref[:, cols] = (gate_ref[:, cols] * out).astype(BF)


def project(at, attended, pieces, gate):
    rows = attended[0].shape[0]
    width = pieces[0].shape[0]
    vmem = pl.BlockSpec(memory_space=pltpu.VMEM)
    return pl.pallas_call(
        project_kernel,
        out_shape=jax.ShapeDtypeStruct((rows, 4 * HALF), BF),
        in_specs=[pl.BlockSpec(memory_space=pltpu.SMEM)] + [vmem] * 9,
        out_specs=vmem,
        scratch_shapes=[pltpu.VMEM((rows, width), BF)],
        compiler_params=pltpu.CompilerParams(vmem_limit_bytes=24 << 20),
        cost_estimate=cost(2 * rows * width * 4 * HALF, width * 4 * HALF * 2 + rows * width * 4),
        name="project",
    )(at, *attended, *pieces, gate.reshape(1, -1))


def shards(tokens, shift, scale, gate, qkv_weight, out_weight, q_gain, k_gain):
    frames, tile_h, tile_w, width = tokens.shape
    count = frames * tile_h * tile_w
    x, l, z, u, c = (lax.axis_index(a) for a in AXES)
    parity = lax.rem(x, 2)
    h = x * 2 + l
    w = z * 2 + u

    parts = [qkv_weight[:, width : 2 * width], qkv_weight[:, 2 * width :], qkv_weight[:, :width], out_weight]
    mine = jnp.concatenate(
        [lax.dynamic_slice_in_dim(m, (c * 2 + parity) * HALF, HALF, 1) for m in parts], axis=1
    )
    theirs = jnp.concatenate(
        [lax.dynamic_slice_in_dim(m, ((1 - c) * 2 + parity) * HALF, HALF, 1) for m in parts], axis=1
    )
    other = send(theirs, SIBLING)
    pair = jnp.where(c == 0, jnp.concatenate([mine, other]), jnp.concatenate([other, mine]))
    other = send(pair, Y_FLIP)
    quad = jnp.where(u == 0, jnp.concatenate([pair, other]), jnp.concatenate([other, pair]))
    wk, wv, wq, wo = (
        lax.all_gather(quad[:, i * HALF : (i + 1) * HALF], "z", axis=0, tiled=True) for i in range(4)
    )
    wk2, wv2 = send(wk, X_DOWN), send(wv, X_UP)
    wq2, wo2 = send(wq, X_DOWN), send(wo, X_UP)
    wo3, wo4 = send(wo, SIBLING), send(wo2, SIBLING)

    own = modulate(tokens.reshape(count, width), scale, shift)
    below, above = send(own, H_UP), send(own, H_DOWN)
    side, side_below, side_above = send(own, SIDE), send(own, SIDE_UP), send(own, SIDE_DOWN)
    outer = [side_below, side, side_above]
    inner = [below, own, above]
    inner2 = [send(t, SIBLING) for t in inner]
    outer2 = [send(t, SIBLING) for t in outer]
    tiles = outer + inner + inner2 + outer2

    col_ok = [jnp.where(c == 0, w > 0, w < 15), True, True, jnp.where(c == 0, w < 15, w > 0)]
    row_ok = [h > 0, True, h < 7]
    far = jnp.stack([jnp.where(jnp.logical_and(a, b), 0.0, FAR).astype(F32) for a in col_ok for b in row_ok])

    q_gain, k_gain = q_gain.reshape(1, HD), k_gain.reshape(1, HD)
    k, v = keys_values(tiles, wk, wv, k_gain)
    q = queries(own, inner2[1], wq, q_gain)
    first = attend(far, q, k, v)
    first2 = send(first[1], SIBLING)
    k, v = keys_values(tiles, wk2, wv2, k_gain)
    q = queries(own, inner2[1], wq2, q_gain)
    second = attend(far, q, k, v)
    second2 = send(second[1], SIBLING)

    at = jnp.stack([c * 2 + parity, c * 2 + 1 - parity, (1 - c) * 2 + parity, (1 - c) * 2 + 1 - parity])
    out = project(at.astype(jnp.int32), [first[0], second[0], first2, second2], [wo, wo2, wo3, wo4], gate)
    return out.reshape(frames, tile_h, tile_w, width)


def solution(mesh):
    fine = Mesh(mesh.devices.reshape(SIZES), AXES)
    tile = P(None, ("x", "l"), ("z", "u", "c"), None)
    rows = P(("z", "u", "c"), None)
    return jax.shard_map(
        shards,
        mesh=fine,
        in_specs=(tile, P(), P(), P(), rows, rows, P(), P()),
        out_specs=tile,
        check_vma=False,
    )
```

```python
import functools

import jax
import jax.numpy as jnp
from jax import lax
from jax.experimental import pallas as pl
from jax.experimental.pallas import tpu as pltpu
from jax.sharding import Mesh
from jax.sharding import PartitionSpec as P

HEADS = 12
HD = 128
TILE_T = 4
EPS = 1e-06
HALF = 3 * HD
AXES = ("x", "l", "z", "u", "c")
SIZES = (4, 2, 8, 2, 2)
FAR = 1e30
BF = jnp.bfloat16
F32 = jnp.float32


def hops(move):
    pairs = []
    for x in range(4):
        for l in range(2):
            for z in range(8):
                for u in range(2):
                    for c in range(2):
                        h, s = (x * 2 + l, (z * 2 + u) * 2 + c)
                        h2, s2 = move(h, s)
                        pairs.append((h * 32 + s, h2 % 8 * 32 + s2 % 32))
    return pairs


def across(s):
    return s + 1 if s % 2 else s - 1


def flip_y(h, s):
    return (h ^ 1, s ^ 2)


SIBLING = hops(lambda h, s: (h, s ^ 1))
H_UP = hops(lambda h, s: (h + 1, s))
H_DOWN = hops(lambda h, s: (h - 1, s))
SIDE = hops(lambda h, s: (h, across(s)))
SIDE_UP = hops(lambda h, s: (h + 1, across(s)))
SIDE_DOWN = hops(lambda h, s: (h - 1, across(s)))
Y_FLIP = hops(flip_y)
X_UP = hops(lambda h, s: (h + 2, s))
X_DOWN = hops(lambda h, s: (h - 2, s))


def send(x, pairs):
    return lax.ppermute(x, AXES, pairs)


def cost(flops, nbytes, trans=0):
    return pl.CostEstimate(flops=int(flops), bytes_accessed=int(nbytes), transcendentals=int(trans))


def modulate_kernel(x_ref, scale_ref, shift_ref, o_ref):
    x = x_ref[...].astype(F32)
    mean = jnp.mean(x, axis=-1, keepdims=True)
    centred = x - mean
    var = jnp.mean(centred * centred, axis=-1, keepdims=True)
    normed = centred * lax.rsqrt(var + EPS)
    o_ref[...] = (normed * (1.0 + scale_ref[...]) + shift_ref[...]).astype(BF)


def modulate(x, scale, shift):
    rows, width = x.shape
    step = 64
    return pl.pallas_call(
        modulate_kernel,
        out_shape=jax.ShapeDtypeStruct((rows, width), BF),
        grid=(rows // step,),
        in_specs=[
            pl.BlockSpec((step, width), lambda i: (i, 0)),
            pl.BlockSpec((1, width), lambda i: (0, 0)),
            pl.BlockSpec((1, width), lambda i: (0, 0)),
        ],
        out_specs=pl.BlockSpec((step, width), lambda i: (i, 0)),
        cost_estimate=cost(rows * width * 8, rows * width * 4),
        name="modulate",
    )(x, scale.reshape(1, -1), shift.reshape(1, -1))


def head_norm(raw, gain):
    return (raw * lax.rsqrt(jnp.mean(raw * raw, axis=-1, keepdims=True) + EPS) * gain).astype(BF)


def qkv_kernel(n, m, mine, at_ref, *refs):
    tiles, blocks = (refs[:n], refs[n : n + m])
    qg_ref, kg_ref, q_ref, k_ref, v_ref, buf, weight, sem, wsem = refs[n + m :]
    i = pl.program_id(0)
    deep = weight.shape[0] // m

    def copies():
        for j, block in enumerate(blocks):
            rows = pl.ds(pl.multiple_of(at_ref[j] * deep, deep), deep)
            yield pltpu.make_async_copy(block, weight.at[rows], wsem.at[j])

    def fetch(j, slot):
        for t in range(n):

            @pl.when(j == t)
            def _():
                pltpu.make_async_copy(tiles[t], buf.at[slot], sem.at[slot]).start()

    @pl.when(i == 0)
    def _():
        for copy in copies():
            copy.start()
        fetch(i, 0)
        for copy in copies():
            copy.wait()

    slot = lax.rem(i, 2)

    @pl.when(i + 1 < n)
    def _():
        fetch(i + 1, 1 - slot)

    pltpu.make_async_copy(tiles[0], buf.at[slot], sem.at[slot]).wait()
    x = buf[slot]
    raw = jnp.dot(x, weight[:, : 2 * HALF], preferred_element_type=F32)
    for h in range(3):
        k_ref[h] = head_norm(raw[:, h * HD : (h + 1) * HD], kg_ref[...])
        v_ref[h] = raw[:, HALF + h * HD : HALF + (h + 1) * HD].astype(BF)

    @pl.when(jnp.logical_or(i == mine[0], i == mine[1]))
    def _():
        t = jnp.where(i == mine[0], 0, 1)
        raw = jnp.dot(buf[slot], weight[:, 2 * HALF :], preferred_element_type=F32)
        for h in range(3):
            q_ref[t, h] = head_norm(raw[:, h * HD : (h + 1) * HD], qg_ref[...])


def project_in(at, tiles, blocks, q_gain, k_gain, mine):
    n, m = (len(tiles), len(blocks))
    rows, width = tiles[0].shape
    hbm = pl.BlockSpec(memory_space=pltpu.HBM)
    return pl.pallas_call(
        functools.partial(qkv_kernel, n, m, mine),
        out_shape=[jax.ShapeDtypeStruct((2, 3, rows, HD), BF)]
        + [jax.ShapeDtypeStruct((3, n * rows, HD), BF)] * 2,
        grid=(n,),
        in_specs=[pl.BlockSpec(memory_space=pltpu.SMEM)]
        + [hbm] * (n + m)
        + [pl.BlockSpec((1, HD), lambda i: (0, 0))] * 2,
        out_specs=[pl.BlockSpec((2, 3, rows, HD), lambda i: (0, 0, 0, 0))]
        + [pl.BlockSpec((3, rows, HD), lambda i: (0, i, 0))] * 2,
        scratch_shapes=[
            pltpu.VMEM((2, rows, width), BF),
            pltpu.VMEM((width, 3 * HALF), BF),
            pltpu.SemaphoreType.DMA((2,)),
            pltpu.SemaphoreType.DMA((m,)),
        ],
        compiler_params=pltpu.CompilerParams(vmem_limit_bytes=20 << 20),
        cost_estimate=cost(
            2 * (n * 2 + 2) * rows * width * HALF, (n * rows * (width + 2 * HALF) + width * 3 * HALF) * 2
        ),
        name="project_in",
    )(at, *tiles, *blocks, q_gain, k_gain)


def attend_kernel(far_ref, q_ref, k_ref, v_ref, o_ref):
    tile = pl.program_id(1)
    rows = q_ref.shape[2]
    q = q_ref[0, 0]
    factor = 1.4426950408889634 / jnp.sqrt(F32(HD))
    base = tile * 3
    scores, top = ([], None)
    for j in range(9):
        at = pl.multiple_of((base + j) * rows, rows)
        k = k_ref[0, pl.ds(at, rows), :]
        s = lax.dot_general(q, k, (((1,), (1,)), ((), ())), preferred_element_type=F32)
        scores.append(s)
        most = jnp.max(s, axis=-1, keepdims=True) - far_ref[base + j]
        top = most if top is None else jnp.maximum(top, most)
    total = jnp.zeros((rows, 1), F32)
    acc = jnp.zeros((rows, HD), F32)
    for j in range(9):
        at = pl.multiple_of((base + j) * rows, rows)
        expo = jnp.exp2((scores[j] - (top + far_ref[base + j])) * factor)
        total += jnp.sum(expo, axis=-1, keepdims=True)
        acc += jnp.dot(expo.astype(BF), v_ref[0, pl.ds(at, rows), :], preferred_element_type=F32)
    o_ref[0] = (acc / total).astype(BF)


def attend(far, q, k, v):
    rows = q.shape[2]
    keys = k.shape[1]
    window = 9 * rows
    return pl.pallas_call(
        attend_kernel,
        out_shape=jax.ShapeDtypeStruct((2, rows, HALF), BF),
        grid_spec=pltpu.PrefetchScalarGridSpec(
            num_scalar_prefetch=1,
            grid=(3, 2),
            in_specs=[
                pl.BlockSpec((1, 1, rows, HD), lambda h, t, far: (t, h, 0, 0)),
                pl.BlockSpec((1, keys, HD), lambda h, t, far: (h, 0, 0)),
                pl.BlockSpec((1, keys, HD), lambda h, t, far: (h, 0, 0)),
            ],
            out_specs=pl.BlockSpec((1, rows, HD), lambda h, t, far: (t, 0, h)),
        ),
        compiler_params=pltpu.CompilerParams(vmem_limit_bytes=20 << 20),
        cost_estimate=cost(6 * rows * window * HD * 4, 6 * keys * HD * 2 * 2, 6 * rows * window),
        name="attend",
    )(far, q, k, v)


def project_kernel(c_ref, at_ref, a0, a1, a2, a3, w0, w1, gate_ref, o_ref, left):
    for j, a in enumerate((a0, a1, a2, a3)):
        left[:, pl.ds(pl.multiple_of(at_ref[j] * HALF, HD), HALF)] = a[...]
    for j, w in enumerate((w0, w1)):
        side = c_ref[0] if j == 0 else 1 - c_ref[0]
        cols = pl.ds(pl.multiple_of(side * 2 * HALF, HD), 2 * HALF)
        out = jnp.dot(left[...], w[...], preferred_element_type=F32)
        o_ref[:, cols] = (gate_ref[:, cols] * out).astype(BF)


def project_out(c, at, attended, pieces, gate):
    rows = attended[0].shape[0]
    width = pieces[0].shape[0]
    vmem = pl.BlockSpec(memory_space=pltpu.VMEM)
    return pl.pallas_call(
        project_kernel,
        out_shape=jax.ShapeDtypeStruct((rows, 4 * HALF), BF),
        in_specs=[pl.BlockSpec(memory_space=pltpu.SMEM)] * 2 + [vmem] * 7,
        out_specs=vmem,
        scratch_shapes=[pltpu.VMEM((rows, width), BF)],
        compiler_params=pltpu.CompilerParams(vmem_limit_bytes=24 << 20),
        cost_estimate=cost(2 * rows * width * 4 * HALF, width * 4 * HALF * 2 + rows * width * 4),
        name="project_out",
    )(c, at, *attended, *pieces, gate.reshape(1, -1))


def shards(tokens, shift, scale, gate, qkv_weight, out_weight, q_gain, k_gain):
    frames, tile_h, tile_w, width = tokens.shape
    count = frames * tile_h * tile_w
    x, l, z, u, c = (lax.axis_index(a) for a in AXES)
    parity = lax.rem(x, 2)
    h = x * 2 + l
    w = z * 2 + u

    def columns(core):
        at = (core * 2 + parity) * HALF
        parts = [lax.dynamic_slice_in_dim(qkv_weight, i * width + at, HALF, 1) for i in (1, 2, 0)]
        parts.append(lax.dynamic_slice_in_dim(out_weight, core * 2 * HALF, 2 * HALF, 1))
        return jnp.concatenate(parts, axis=1)

    mine, other = columns(c), send(columns(1 - c), SIBLING)
    pair = jnp.where(c == 0, jnp.concatenate([mine, other]), jnp.concatenate([other, mine]))
    other = send(pair, Y_FLIP)
    flat, pair = lax.optimization_barrier((tokens.reshape(count, width), pair))
    own = modulate(flat, scale, shift)
    own, other = lax.optimization_barrier((own, other))
    quad = jnp.where(u == 0, jnp.concatenate([pair, other]), jnp.concatenate([other, pair]))
    w_in = lax.all_gather(quad[:, : 3 * HALF], "z", axis=0, tiled=True)
    w_out = lax.all_gather(quad[:, 3 * HALF :], "z", axis=0, tiled=True)
    w_in2 = [send(w_in[: width // 2], X_DOWN), send(w_in[width // 2 :], X_UP)]

    below, above = send(own, H_UP), send(own, H_DOWN)
    side, side_below, side_above = send(own, SIDE), send(own, SIDE_UP), send(own, SIDE_DOWN)
    outer = [side_below, side, side_above]
    inner = [below, own, above]
    inner2 = [send(t, SIBLING) for t in inner]
    outer2 = [send(t, SIBLING) for t in outer]
    tiles = outer + inner + inner2 + outer2

    col_ok = [jnp.where(c == 0, w > 0, w < 15), True, True, jnp.where(c == 0, w < 15, w > 0)]
    row_ok = [h > 0, True, h < 7]
    far = jnp.stack([jnp.where(jnp.logical_and(a, b), 0.0, FAR).astype(F32) for a in col_ok for b in row_ok])

    gains = (q_gain.reshape(1, HD), k_gain.reshape(1, HD))
    q, k, v = project_in(jnp.arange(1, dtype=jnp.int32), tiles, [w_in], *gains, (4, 7))
    first = attend(far, q, k, v)
    first2 = send(first[1], SIBLING)
    q, k, v = project_in(jnp.arange(2, dtype=jnp.int32), tiles, w_in2, *gains, (4, 7))
    q, w_out = lax.optimization_barrier((q, w_out))
    w_out2 = send(w_out, SIBLING)
    second = attend(far, q, k, v)
    second2 = send(second[1], SIBLING)

    at = jnp.stack([c * 2 + parity, c * 2 + 1 - parity, (1 - c) * 2 + parity, (1 - c) * 2 + 1 - parity])
    attended = [first[0], second[0], first2, second2]
    out = project_out(c.reshape(1), at.astype(jnp.int32), attended, [w_out, w_out2], gate)
    return out.reshape(frames, tile_h, tile_w, width)


def solution(mesh):
    fine = Mesh(mesh.devices.reshape(SIZES), AXES)
    tile = P(None, ("x", "l"), ("z", "u", "c"), None)
    rows = P(("z", "u", "c"), None)
    return jax.shard_map(
        shards,
        mesh=fine,
        in_specs=(tile, P(), P(), P(), rows, rows, P(), P()),
        out_specs=tile,
        check_vma=False,
    )
```

```python
import functools

import jax
import jax.numpy as jnp
from jax import lax
from jax.experimental import pallas as pl
from jax.experimental.pallas import tpu as pltpu
from jax.sharding import Mesh
from jax.sharding import PartitionSpec as P

HEADS = 12
HD = 128
TILE_T = 4
EPS = 1e-06
HALF = 3 * HD
AXES = ("x", "l", "z", "u", "c")
SIZES = (4, 2, 8, 2, 2)
FAR = 1e30
BF = jnp.bfloat16
F32 = jnp.float32


def hops(move):
    pairs = []
    for x in range(4):
        for l in range(2):
            for z in range(8):
                for u in range(2):
                    for c in range(2):
                        h, s = (x * 2 + l, (z * 2 + u) * 2 + c)
                        h2, s2 = move(h, s)
                        pairs.append((h * 32 + s, h2 % 8 * 32 + s2 % 32))
    return pairs


def across(s):
    return s + 1 if s % 2 else s - 1


def flip_y(h, s):
    return (h ^ 1, s ^ 2)


SIBLING = hops(lambda h, s: (h, s ^ 1))
H_UP = hops(lambda h, s: (h + 1, s))
H_DOWN = hops(lambda h, s: (h - 1, s))
SIDE = hops(lambda h, s: (h, across(s)))
SIDE_UP = hops(lambda h, s: (h + 1, across(s)))
SIDE_DOWN = hops(lambda h, s: (h - 1, across(s)))
Y_FLIP = hops(flip_y)
X_UP = hops(lambda h, s: (h + 2, s))
X_DOWN = hops(lambda h, s: (h - 2, s))


def send(x, pairs):
    return lax.ppermute(x, AXES, pairs)


def cost(flops, nbytes, trans=0):
    return pl.CostEstimate(flops=int(flops), bytes_accessed=int(nbytes), transcendentals=int(trans))


def modulate_kernel(x_ref, scale_ref, shift_ref, o_ref):
    x = x_ref[...].astype(F32)
    mean = jnp.mean(x, axis=-1, keepdims=True)
    centred = x - mean
    var = jnp.mean(centred * centred, axis=-1, keepdims=True)
    normed = centred * lax.rsqrt(var + EPS)
    o_ref[...] = (normed * (1.0 + scale_ref[...]) + shift_ref[...]).astype(BF)


def modulate(x, scale, shift):
    rows, width = x.shape
    step = 64
    return pl.pallas_call(
        modulate_kernel,
        out_shape=jax.ShapeDtypeStruct((rows, width), BF),
        grid=(rows // step,),
        in_specs=[
            pl.BlockSpec((step, width), lambda i: (i, 0)),
            pl.BlockSpec((1, width), lambda i: (0, 0)),
            pl.BlockSpec((1, width), lambda i: (0, 0)),
        ],
        out_specs=pl.BlockSpec((step, width), lambda i: (i, 0)),
        cost_estimate=cost(rows * width * 8, rows * width * 4),
        name="modulate",
    )(x, scale.reshape(1, -1), shift.reshape(1, -1))


def head_norm(raw, gain):
    return (raw * lax.rsqrt(jnp.mean(raw * raw, axis=-1, keepdims=True) + EPS) * gain).astype(BF)


def qkv_kernel(n, m, order_ref, at_ref, *refs):
    tiles, blocks = (refs[:n], refs[n : n + m])
    qg_ref, kg_ref, q_ref, k_ref, v_ref, buf, weight, sem, wsem = refs[n + m :]
    i = pl.program_id(0)
    deep = weight.shape[0] // m
    rows = buf.shape[1] // 2

    def copies():
        for j, block in enumerate(blocks):
            to = pl.ds(pl.multiple_of(at_ref[j] * deep, deep), deep)
            yield pltpu.make_async_copy(block, weight.at[to], wsem.at[j])

    def fetch(step, slot):
        for part in range(2):
            which = order_ref[step * 2 + part]
            for t in range(n):

                @pl.when(which == t)
                def _():
                    to = buf.at[slot, pl.ds(part * rows, rows)]
                    pltpu.make_async_copy(tiles[t], to, sem.at[slot, part]).start()

    @pl.when(i == 0)
    def _():
        fetch(i, 0)
        for copy in copies():
            copy.start()
        for copy in copies():
            copy.wait()

    slot = lax.rem(i, 2)

    @pl.when(i + 1 < n // 2)
    def _():
        fetch(i + 1, 1 - slot)

    for part in range(2):
        to = buf.at[slot, pl.ds(part * rows, rows)]
        pltpu.make_async_copy(tiles[0], to, sem.at[slot, part]).wait()
    x = buf[slot]
    raw = jnp.dot(x, weight[:, : 2 * HALF], preferred_element_type=F32)
    for h in range(3):
        k_ref[h] = head_norm(raw[:, h * HD : (h + 1) * HD], kg_ref[...])
        v_ref[h] = raw[:, HALF + h * HD : HALF + (h + 1) * HD].astype(BF)

    for t, slots in enumerate((4, 7)):

        @pl.when(i == slots // 2)
        def _():
            x = buf[slot, pl.ds(slots % 2 * rows, rows)]
            raw = jnp.dot(x, weight[:, 2 * HALF :], preferred_element_type=F32)
            for h in range(3):
                q_ref[t, h] = head_norm(raw[:, h * HD : (h + 1) * HD], qg_ref[...])


def project_in(order, at, tiles, blocks, q_gain, k_gain):
    n, m = (len(tiles), len(blocks))
    rows, width = tiles[0].shape
    hbm = pl.BlockSpec(memory_space=pltpu.HBM)
    return pl.pallas_call(
        functools.partial(qkv_kernel, n, m),
        out_shape=[jax.ShapeDtypeStruct((2, 3, rows, HD), BF)]
        + [jax.ShapeDtypeStruct((3, n * rows, HD), BF)] * 2,
        grid=(n // 2,),
        in_specs=[pl.BlockSpec(memory_space=pltpu.SMEM)] * 2
        + [hbm] * (n + m)
        + [pl.BlockSpec((1, HD), lambda i: (0, 0))] * 2,
        out_specs=[pl.BlockSpec((2, 3, rows, HD), lambda i: (0, 0, 0, 0))]
        + [pl.BlockSpec((3, 2 * rows, HD), lambda i: (0, i, 0))] * 2,
        scratch_shapes=[
            pltpu.VMEM((2, 2 * rows, width), BF),
            pltpu.VMEM((width, 3 * HALF), BF),
            pltpu.SemaphoreType.DMA((2, 2)),
            pltpu.SemaphoreType.DMA((m,)),
        ],
        compiler_params=pltpu.CompilerParams(vmem_limit_bytes=60 << 20),
        cost_estimate=cost(
            2 * (n * 2 + 2) * rows * width * HALF, (n * rows * (width + 2 * HALF) + width * 3 * HALF) * 2
        ),
        name="project_in",
    )(order, at, *tiles, *blocks, q_gain, k_gain)


def attend_kernel(far_ref, q_ref, k_ref, v_ref, o_ref):
    tile = pl.program_id(1)
    rows = q_ref.shape[2]
    q = q_ref[0, 0]
    factor = 1.4426950408889634 / jnp.sqrt(F32(HD))
    base = tile * 3
    scores, top = ([], None)
    for j in range(9):
        at = pl.multiple_of((base + j) * rows, rows)
        k = k_ref[0, pl.ds(at, rows), :]
        s = lax.dot_general(q, k, (((1,), (1,)), ((), ())), preferred_element_type=F32)
        scores.append(s)
        most = jnp.max(s, axis=-1, keepdims=True) - far_ref[base + j]
        top = most if top is None else jnp.maximum(top, most)
    total = jnp.zeros((rows, 1), F32)
    acc = jnp.zeros((rows, HD), F32)
    for j in range(9):
        at = pl.multiple_of((base + j) * rows, rows)
        expo = jnp.exp2((scores[j] - (top + far_ref[base + j])) * factor)
        total += jnp.sum(expo, axis=-1, keepdims=True)
        acc += jnp.dot(expo.astype(BF), v_ref[0, pl.ds(at, rows), :], preferred_element_type=F32)
    o_ref[0] = (acc / total).astype(BF)


def attend(far, q, k, v):
    rows = q.shape[2]
    keys = k.shape[1]
    window = 9 * rows
    return pl.pallas_call(
        attend_kernel,
        out_shape=jax.ShapeDtypeStruct((2, rows, HALF), BF),
        grid_spec=pltpu.PrefetchScalarGridSpec(
            num_scalar_prefetch=1,
            grid=(3, 2),
            in_specs=[
                pl.BlockSpec((1, 1, rows, HD), lambda h, t, far: (t, h, 0, 0)),
                pl.BlockSpec((1, keys, HD), lambda h, t, far: (h, 0, 0)),
                pl.BlockSpec((1, keys, HD), lambda h, t, far: (h, 0, 0)),
            ],
            out_specs=pl.BlockSpec((1, rows, HD), lambda h, t, far: (t, 0, h)),
        ),
        compiler_params=pltpu.CompilerParams(vmem_limit_bytes=60 << 20),
        cost_estimate=cost(6 * rows * window * HD * 4, 6 * keys * HD * 2 * 2, 6 * rows * window),
        name="attend",
    )(far, q, k, v)


def project_kernel(c_ref, at_ref, a0, a1, a2, a3, w0, w1, gate_ref, o_ref, left):
    for j, a in enumerate((a0, a1, a2, a3)):
        left[:, pl.ds(pl.multiple_of(at_ref[j] * HALF, HD), HALF)] = a[...]
    for j, w in enumerate((w0, w1)):
        side = c_ref[0] if j == 0 else 1 - c_ref[0]
        cols = pl.ds(pl.multiple_of(side * 2 * HALF, HD), 2 * HALF)
        out = jnp.dot(left[...], w[...], preferred_element_type=F32)
        o_ref[:, cols] = (gate_ref[:, cols] * out).astype(BF)


def project_out(c, at, attended, pieces, gate):
    rows = attended[0].shape[0]
    width = pieces[0].shape[0]
    vmem = pl.BlockSpec(memory_space=pltpu.VMEM)
    return pl.pallas_call(
        project_kernel,
        out_shape=jax.ShapeDtypeStruct((rows, 4 * HALF), BF),
        in_specs=[pl.BlockSpec(memory_space=pltpu.SMEM)] * 2 + [vmem] * 7,
        out_specs=vmem,
        scratch_shapes=[pltpu.VMEM((rows, width), BF)],
        compiler_params=pltpu.CompilerParams(vmem_limit_bytes=16 << 20),
        cost_estimate=cost(2 * rows * width * 4 * HALF, width * 4 * HALF * 2 + rows * width * 4),
        name="project_out",
    )(c, at, *attended, *pieces, gate.reshape(1, -1))


def shards(tokens, shift, scale, gate, qkv_weight, out_weight, q_gain, k_gain):
    frames, tile_h, tile_w, width = tokens.shape
    count = frames * tile_h * tile_w
    x, l, z, u, c = (lax.axis_index(a) for a in AXES)
    parity = lax.rem(x, 2)
    h = x * 2 + l
    w = z * 2 + u

    def columns(core):
        at = (core * 2 + parity) * HALF
        parts = [lax.dynamic_slice_in_dim(qkv_weight, i * width + at, HALF, 1) for i in (1, 2, 0)]
        parts.append(lax.dynamic_slice_in_dim(out_weight, core * 2 * HALF, 2 * HALF, 1))
        return jnp.concatenate(parts, axis=1)

    mine, other = columns(c), send(columns(1 - c), SIBLING)
    pair = jnp.where(c == 0, jnp.concatenate([mine, other]), jnp.concatenate([other, mine]))
    other = send(pair, Y_FLIP)
    flat, pair = lax.optimization_barrier((tokens.reshape(count, width), pair))
    own = modulate(flat, scale, shift)
    own, other = lax.optimization_barrier((own, other))
    quad = jnp.where(u == 0, jnp.concatenate([pair, other]), jnp.concatenate([other, pair]))
    w_in = lax.all_gather(quad[:, : 3 * HALF], "z", axis=0, tiled=True)
    w_out = lax.all_gather(quad[:, 3 * HALF :], "z", axis=0, tiled=True)
    w_in2 = [send(w_in[: width // 2], X_DOWN), send(w_in[width // 2 :], X_UP)]

    below, above = send(own, H_UP), send(own, H_DOWN)
    side, side_below, side_above = send(own, SIDE), send(own, SIDE_UP), send(own, SIDE_DOWN)
    outer = [side_below, side, side_above]
    inner = [below, own, above]
    inner2 = [send(t, SIBLING) for t in inner]
    outer2 = [send(t, SIBLING) for t in outer]
    tiles = outer + inner + inner2 + outer2

    col_ok = [jnp.where(c == 0, w > 0, w < 15), True, True, jnp.where(c == 0, w < 15, w > 0)]
    row_ok = [h > 0, True, h < 7]
    far = jnp.stack([jnp.where(jnp.logical_and(a, b), 0.0, FAR).astype(F32) for a in col_ok for b in row_ok])

    gains = (q_gain.reshape(1, HD), k_gain.reshape(1, HD))
    order = jnp.arange(12, dtype=jnp.int32)
    q, k, v = project_in(order, jnp.arange(1, dtype=jnp.int32), tiles, [w_in], *gains)
    first = attend(far, q, k, v)
    first2 = send(first[1], SIBLING)
    first, *w_in2 = lax.optimization_barrier((first, *w_in2))
    q, k, v = project_in(order, jnp.arange(2, dtype=jnp.int32), tiles, w_in2, *gains)
    q, w_out = lax.optimization_barrier((q, w_out))
    w_out2 = send(w_out, SIBLING)
    second = attend(far, q, k, v)
    second2 = send(second[1], SIBLING)

    at = jnp.stack([c * 2 + parity, c * 2 + 1 - parity, (1 - c) * 2 + parity, (1 - c) * 2 + 1 - parity])
    attended = [first[0], second[0], first2, second2]
    out = project_out(c.reshape(1), at.astype(jnp.int32), attended, [w_out, w_out2], gate)
    return out.reshape(frames, tile_h, tile_w, width)


def solution(mesh):
    fine = Mesh(mesh.devices.reshape(SIZES), AXES)
    tile = P(None, ("x", "l"), ("z", "u", "c"), None)
    rows = P(("z", "u", "c"), None)
    return jax.shard_map(
        shards,
        mesh=fine,
        in_specs=(tile, P(), P(), P(), rows, rows, P(), P()),
        out_specs=tile,
        check_vma=False,
    )
```

```python
import functools
import itertools

import jax
import jax.numpy as jnp
from jax import lax
from jax.experimental import pallas as pl
from jax.experimental.pallas import tpu as pltpu
from jax.sharding import Mesh
from jax.sharding import PartitionSpec as P

HEADS = 12
HD = 128
TILE_T = 4
EPS = 1e-06
HALF = 3 * HD
AXES = ("x", "l", "z", "u", "c")
SIZES = (4, 2, 8, 2, 2)
FAR = 1e30
BF = jnp.bfloat16
F32 = jnp.float32


def hops(move):
    pairs = []
    for x, l, z, u, c in itertools.product(*map(range, SIZES)):
        x2, y2, z2, c2 = move(x, u * 2 + l, z, c)
        to = (x2 % 4, y2 % 2, z2 % 8, y2 // 2, c2)
        rank = [functools.reduce(lambda r, d: r * d[0] + d[1], zip(SIZES, at), 0) for at in ((x, l, z, u, c), to)]
        pairs.append(tuple(rank))
    return pairs


def tile_hop(down, across):
    def move(x, y, z, c):
        h, w = ((x * 2 + y % 2 + down) % 8, (z * 2 + y // 2 + across[c]) % 16)
        return h // 2, w % 2 * 2 + h % 2, w // 2, c

    return hops(move)


SIBLING = hops(lambda x, y, z, c: (x, y, z, 1 - c))
Y_FLIP = hops(lambda x, y, z, c: (x, 3 - y, z, c))
X_A = hops(lambda x, y, z, c: (x + 1 - 2 * c, y, z, c))
X_B = hops(lambda x, y, z, c: (x - 1 + 2 * c, y, z, c))
Z_A = hops(lambda x, y, z, c: (x, y, z + 1 - 2 * c, c))
Z_B = hops(lambda x, y, z, c: (x, y, z - 1 + 2 * c, c))
Z_A2 = hops(lambda x, y, z, c: (x, y, z + 2 - 4 * c, c))
Z_B2 = hops(lambda x, y, z, c: (x, y, z - 2 + 4 * c, c))
TOKENS = (
    tile_hop(1, (0, 1)),
    tile_hop(1, (-1, 0)),
    tile_hop(-1, (0, 1)),
    tile_hop(-1, (-1, 0)),
    tile_hop(0, (-1, 1)),
)
ORDER = ((7, 11, 9, 1, 0, 3, 8, 6, 10, 2, 5, 4), (8, 11, 10, 2, 0, 4, 7, 6, 9, 1, 5, 3))
RING = (0, -1, 1, -2, 2, -3, 3, -4)


def send(x, pairs):
    return lax.ppermute(x, AXES, pairs)


def together(*values):
    return lax.optimization_barrier(values)


def cost(flops, nbytes, trans=0):
    return pl.CostEstimate(flops=int(flops), bytes_accessed=int(nbytes), transcendentals=int(trans))


def modulate_kernel(x_ref, scale_ref, shift_ref, o_ref):
    x = x_ref[...].astype(F32)
    mean = jnp.mean(x, axis=-1, keepdims=True)
    centred = x - mean
    var = jnp.mean(centred * centred, axis=-1, keepdims=True)
    normed = centred * lax.rsqrt(var + EPS)
    o_ref[...] = (normed * (1.0 + scale_ref[...]) + shift_ref[...]).astype(BF)


def modulate(x, scale, shift):
    rows, width = x.shape
    step = 64
    return pl.pallas_call(
        modulate_kernel,
        out_shape=jax.ShapeDtypeStruct((rows, width), BF),
        grid=(rows // step,),
        in_specs=[
            pl.BlockSpec((step, width), lambda i: (i, 0)),
            pl.BlockSpec((1, width), lambda i: (0, 0)),
            pl.BlockSpec((1, width), lambda i: (0, 0)),
        ],
        out_specs=pl.BlockSpec((step, width), lambda i: (i, 0)),
        cost_estimate=cost(rows * width * 8, rows * width * 4),
        name="modulate",
    )(x, scale.reshape(1, -1), shift.reshape(1, -1))


def head_norm(raw, gain):
    return (raw * lax.rsqrt(jnp.mean(raw * raw, axis=-1, keepdims=True) + EPS) * gain).astype(BF)


def heads_kernel(n, m, order_ref, at_ref, far_ref, *refs):
    tiles, blocks = (refs[:n], refs[n : n + m])
    qg_ref, kg_ref, mine_ref, theirs_ref, buf, weight, q_ref, k_ref, v_ref, sem, wsem = refs[n + m :]
    i = pl.program_id(0)
    deep = weight.shape[0] // m
    rows = buf.shape[1]
    steps = n

    def copies():
        for j, block in enumerate(blocks):
            to = pl.ds(pl.multiple_of(at_ref[j] * deep, deep), deep)
            yield pltpu.make_async_copy(block, weight.at[to], wsem.at[j])

    def fetch(step, slot):
        which = order_ref[step]
        for t in range(n):

            @pl.when(which == t)
            def _():
                pltpu.make_async_copy(tiles[t], buf.at[slot], sem.at[slot]).start()

    @pl.when(i == 0)
    def _():
        fetch(i, 0)
        for copy in copies():
            copy.start()
        for copy in copies():
            copy.wait()

    slot = lax.rem(i, 2)

    @pl.when(i + 1 < steps)
    def _():
        fetch(i + 1, 1 - slot)

    @pl.when(i < steps)
    def _():
        pltpu.make_async_copy(tiles[0], buf.at[slot], sem.at[slot]).wait()
        raw = jnp.dot(buf[slot], weight[:, : 2 * HALF], preferred_element_type=F32)
        at = pl.ds(pl.multiple_of(i * rows, rows), rows)
        for h in range(3):
            k_ref[h, at] = head_norm(raw[:, h * HD : (h + 1) * HD], kg_ref[...])
            v_ref[h, at] = raw[:, HALF + h * HD : HALF + (h + 1) * HD].astype(BF)

    @pl.when(jnp.logical_or(i == 4, i == 7))
    def _():
        t = jnp.where(i == 4, 0, 1)
        raw = jnp.dot(buf[slot], weight[:, 2 * HALF :], preferred_element_type=F32)
        for h in range(3):
            q_ref[t, h] = head_norm(raw[:, h * HD : (h + 1) * HD], qg_ref[...])

    @pl.when(i >= steps)
    def _():
        h, t = ((i - steps) // 2, lax.rem(i - steps, 2))
        q = q_ref[t, h]
        factor = 1.4426950408889634 / jnp.sqrt(F32(HD))
        scores, top = ([], None)
        for j in range(9):
            at = pl.multiple_of((t * 3 + j) * rows, rows)
            k = k_ref[h, pl.ds(at, rows), :]
            s = lax.dot_general(q, k, (((1,), (1,)), ((), ())), preferred_element_type=F32)
            scores.append(s)
            most = jnp.max(s, axis=-1, keepdims=True) - far_ref[t * 3 + j]
            top = most if top is None else jnp.maximum(top, most)
        total = jnp.zeros((rows, 1), F32)
        acc = jnp.zeros((rows, HD), F32)
        for j in range(9):
            at = pl.multiple_of((t * 3 + j) * rows, rows)
            v = v_ref[h, pl.ds(at, rows), :]
            expo = jnp.exp2((scores[j] - (top + far_ref[t * 3 + j])) * factor)
            total += jnp.sum(expo, axis=-1, keepdims=True)
            acc += jnp.dot(expo.astype(BF), v, preferred_element_type=F32)
        result = (acc / total).astype(BF)
        cols = pl.ds(pl.multiple_of(h * HD, HD), HD)

        @pl.when(t == 0)
        def _():
            mine_ref[:, cols] = result

        @pl.when(t == 1)
        def _():
            theirs_ref[:, cols] = result


def three_heads(order, at, far, tiles, blocks, q_gain, k_gain):
    n, m = (len(tiles), len(blocks))
    rows, width = tiles[0].shape
    hbm = pl.BlockSpec(memory_space=pltpu.HBM)
    return pl.pallas_call(
        functools.partial(heads_kernel, n, m),
        out_shape=[jax.ShapeDtypeStruct((rows, HALF), BF)] * 2,
        grid=(n + 6,),
        in_specs=[pl.BlockSpec(memory_space=pltpu.SMEM)] * 3
        + [hbm] * (n + m)
        + [pl.BlockSpec((1, HD), lambda i: (0, 0))] * 2,
        out_specs=[pl.BlockSpec((rows, HALF), lambda i: (0, 0))] * 2,
        scratch_shapes=[
            pltpu.VMEM((2, rows, width), BF),
            pltpu.VMEM((width, 3 * HALF), BF),
            pltpu.VMEM((2, 3, rows, HD), BF),
            pltpu.VMEM((3, n * rows, HD), BF),
            pltpu.VMEM((3, n * rows, HD), BF),
            pltpu.SemaphoreType.DMA((2,)),
            pltpu.SemaphoreType.DMA((m,)),
        ],
        compiler_params=pltpu.CompilerParams(vmem_limit_bytes=60 << 20),
        cost_estimate=cost(
            2 * (n * 2 + 2) * rows * width * HALF + 6 * rows * 9 * rows * HD * 4,
            (n * rows * width + width * 3 * HALF) * 2,
            6 * rows * 9 * rows,
        ),
        name="three_heads",
    )(order, at, far, *tiles, *blocks, q_gain, k_gain)


def stack_kernel(m, *refs):
    blocks, (o_ref, sem) = (refs[:m], refs[m:])
    deep = o_ref.shape[0] // m
    copies = [
        pltpu.make_async_copy(block, o_ref.at[pl.ds(j * deep, deep)], sem.at[j])
        for j, block in enumerate(blocks)
    ]
    for copy in copies:
        copy.start()
    for copy in copies:
        copy.wait()


def stack(blocks):
    m = len(blocks)
    deep, cols = blocks[0].shape
    hbm = pl.BlockSpec(memory_space=pltpu.HBM)
    return pl.pallas_call(
        functools.partial(stack_kernel, m),
        out_shape=jax.ShapeDtypeStruct((m * deep, cols), BF),
        in_specs=[hbm] * m,
        out_specs=hbm,
        scratch_shapes=[pltpu.SemaphoreType.DMA((m,))],
        compiler_params=pltpu.CompilerParams(vmem_limit_bytes=60 << 20),
        cost_estimate=cost(0, m * deep * cols * 4),
        name="stack",
    )(*blocks)


def project_kernel(c_ref, at_ref, mine_ref, theirs_ref, a0, a1, a2, a3, gate_ref, *refs):
    m = len(RING)
    blocks, theirs, (o_ref, left, weight, sem) = (refs[:m], refs[m : m + 4], refs[m + 4 :])
    deep = weight.shape[1] // m
    sources = [(0, mine_ref[j], blocks[j]) for j in range(m)]
    sources += [(1, theirs_ref[j], theirs[0].at[pl.ds(j * deep, deep)]) for j in range(m - 3)]
    sources += [(1, theirs_ref[m - 3 + j], theirs[1 + j]) for j in range(3)]
    copies = [
        pltpu.make_async_copy(ref, weight.at[side, pl.ds(pl.multiple_of(row * deep, deep), deep)], sem.at[j])
        for j, (side, row, ref) in enumerate(sources)
    ]
    for copy in copies:
        copy.start()
    for j, a in enumerate((a0, a1, a2, a3)):
        left[:, pl.ds(pl.multiple_of(at_ref[j] * HALF, HD), HALF)] = a[...]
    for side in range(2):
        for copy in copies[side * m : (side + 1) * m]:
            copy.wait()
        core = c_ref[0] if side == 0 else 1 - c_ref[0]
        cols = pl.ds(pl.multiple_of(core * 2 * HALF, HD), 2 * HALF)
        out = jnp.dot(left[...], weight[side], preferred_element_type=F32)
        o_ref[:, cols] = (gate_ref[:, cols] * out).astype(BF)


def project_out(c, at, rows_at, attended, blocks, theirs, gate):
    rows = attended[0].shape[0]
    width = 4 * HALF
    vmem = pl.BlockSpec(memory_space=pltpu.VMEM)
    smem = pl.BlockSpec(memory_space=pltpu.SMEM)
    hbm = pl.BlockSpec(memory_space=pltpu.HBM)
    return pl.pallas_call(
        project_kernel,
        out_shape=jax.ShapeDtypeStruct((rows, width), BF),
        in_specs=[smem] * 4 + [vmem] * 5 + [hbm] * (len(blocks) + len(theirs)),
        out_specs=vmem,
        scratch_shapes=[
            pltpu.VMEM((rows, width), BF),
            pltpu.VMEM((2, width, 2 * HALF), BF),
            pltpu.SemaphoreType.DMA((2 * len(RING),)),
        ],
        compiler_params=pltpu.CompilerParams(vmem_limit_bytes=60 << 20),
        cost_estimate=cost(2 * rows * width * width, width * width * 2 + rows * width * 4),
        name="project_out",
    )(c, at, *rows_at, *attended, gate.reshape(1, -1), *blocks, *theirs)


def shards(tokens, shift, scale, gate, qkv_weight, out_weight, q_gain, k_gain):
    frames, tile_h, tile_w, width = tokens.shape
    count = frames * tile_h * tile_w
    x, l, z, u, c = (lax.axis_index(a) for a in AXES)
    parity = lax.rem(x, 2)
    h = x * 2 + l
    w = z * 2 + u

    def columns(core):
        at = (core * 2 + parity) * HALF
        parts = [lax.dynamic_slice_in_dim(qkv_weight, i * width + at, HALF, 1) for i in (1, 2, 0)]
        parts.append(lax.dynamic_slice_in_dim(out_weight, core * 2 * HALF, 2 * HALF, 1))
        return jnp.concatenate(parts, axis=1)

    mine, other = columns(c), send(columns(1 - c), SIBLING)
    own = modulate(tokens.reshape(count, width), scale, shift)
    own, other = together(own, other)
    pair = jnp.where(c == 0, jnp.concatenate([mine, other]), jnp.concatenate([other, mine]))
    other, t1, own2, own = together(send(pair, Y_FLIP), send(own, TOKENS[0]), send(own, SIBLING), own)
    first = jnp.where(u == 0, pair, other)
    last = jnp.where(u == 0, other, pair)
    cut = 3 * HALF
    block = jnp.concatenate([first[:, :cut], last[:, :cut]])
    out0 = jnp.concatenate([first[:, cut:], last[:, cut:]])

    a1, b1, x0, t2, s1, own = together(
        send(block, Z_A), send(block, Z_B), send(block, X_B), send(own, TOKENS[1]), send(t1, SIBLING), own
    )
    a2, b2, xa1, xb1, t3, own, t2 = together(
        send(a1, Z_A), send(b1, Z_B), send(a1, X_A), send(b1, X_B), send(own, TOKENS[2]), own, t2
    )
    a3, b3, xa2, xb2, t4, own, t2 = together(
        send(a2, Z_A), send(b2, Z_B), send(a2, X_A), send(b2, X_B), send(own, TOKENS[3]), own, t2
    )
    a4, xa3, xb3, t5, s2, own, t3, t4 = together(
        send(a3, Z_A), send(a3, X_A), send(b3, X_B), send(own, TOKENS[4]), send(t2, SIBLING), own, t3, t4
    )
    s3, s4, s5, a4 = together(send(t3, SIBLING), send(t4, SIBLING), send(t5, SIBLING), a4)
    tiles = [own, t1, t2, t3, t4, t5, own2, s1, s2, s3, s4, s5]
    blocks = [block, a1, b1, a2, b2, a3, b3, a4]

    col_ok = [jnp.where(c == 0, w > 0, w < 15), True, True, jnp.where(c == 0, w < 15, w > 0)]
    row_ok = [h > 0, True, h < 7]
    far = jnp.stack([jnp.where(jnp.logical_and(a, b), 0.0, FAR).astype(F32) for a in col_ok for b in row_ok])
    order = jnp.where(c == 0, jnp.array(ORDER[0], jnp.int32), jnp.array(ORDER[1], jnp.int32))
    ring = jnp.array(RING, jnp.int32)
    rows_at = [(z + (1 - 2 * c) * ring) % 8, (z - (1 - 2 * c) * ring) % 8]
    gains = (q_gain.reshape(1, HD), k_gain.reshape(1, HD))

    a4, out0, own = together(a4, out0, own)
    xa4, oa1, ob1 = send(a4, X_A), send(out0, Z_A), send(out0, Z_B)
    oa2, ob2 = send(out0, Z_A2), send(out0, Z_B2)
    mine1, theirs1 = three_heads(order, rows_at[0], far, tiles, blocks, *gains)
    mine1, theirs1, xa4, oa1, ob1, oa2, ob2 = together(mine1, theirs1, xa4, oa1, ob1, oa2, ob2)

    blocks = [x0, xa1, xb1, xa2, xb2, xa3, xb3, xa4]
    oa3, ob3, oa4 = send(oa2, Z_A), send(ob2, Z_B), send(oa2, Z_A2)
    near = send(stack([out0, oa1, ob1, oa2, ob2]), SIBLING)
    mine3 = send(theirs1, SIBLING)
    mine2, theirs2 = three_heads(order, rows_at[0], far, tiles, blocks, *gains)
    theirs2, mine3, near, oa3, ob3, oa4 = together(theirs2, mine3, near, oa3, ob3, oa4)
    mine4 = send(theirs2, SIBLING)
    others = [near, send(oa3, SIBLING), send(ob3, SIBLING), send(oa4, SIBLING)]

    at = jnp.stack([c * 2 + parity, c * 2 + 1 - parity, (1 - c) * 2 + parity, (1 - c) * 2 + 1 - parity])
    out = project_out(
        c.reshape(1),
        at.astype(jnp.int32),
        rows_at,
        [mine1, mine2, mine3, mine4],
        [out0, oa1, ob1, oa2, ob2, oa3, ob3, oa4],
        others,
        gate,
    )
    return out.reshape(frames, tile_h, tile_w, width)


def solution(mesh):
    fine = Mesh(mesh.devices.reshape(SIZES), AXES)
    tile = P(None, ("x", "l"), ("z", "u", "c"), None)
    rows = P(("z", "u", "c"), None)
    return jax.shard_map(
        shards,
        mesh=fine,
        in_specs=(tile, P(), P(), P(), rows, rows, P(), P()),
        out_specs=tile,
        check_vma=False,
    )
```

```python
import functools
import itertools

import jax
import jax.numpy as jnp
from jax import lax
from jax.experimental import pallas as pl
from jax.experimental.pallas import tpu as pltpu
from jax.sharding import Mesh
from jax.sharding import PartitionSpec as P

HEADS = 12
HD = 128
TILE_T = 4
EPS = 1e-06
HALF = 3 * HD
AXES = ("x", "l", "z", "u", "c")
SIZES = (4, 2, 8, 2, 2)
FAR = 1e30
BF = jnp.bfloat16
F32 = jnp.float32


def hops(move):
    pairs = []
    for x, l, z, u, c in itertools.product(*map(range, SIZES)):
        x2, y2, z2, c2 = move(x, u * 2 + l, z, c)
        to = (x2 % 4, y2 % 2, z2 % 8, y2 % 4 // 2, c2)
        rank = [functools.reduce(lambda r, d: r * d[0] + d[1], zip(SIZES, at), 0) for at in ((x, l, z, u, c), to)]
        pairs.append(tuple(rank))
    return pairs


def tile_hop(down, across):
    def move(x, y, z, c):
        h, w = ((x * 2 + y % 2 + down) % 8, (z * 2 + y // 2 + across[c]) % 16)
        return h // 2, w % 2 * 2 + h % 2, w // 2, c

    return hops(move)


SIBLING = hops(lambda x, y, z, c: (x, y, z, 1 - c))
U_FLIP = hops(lambda x, y, z, c: (x, y + 2, z, c))
NEAR = (
    hops(lambda x, y, z, c: (x + 1, y, z, c)),
    hops(lambda x, y, z, c: (x - 1, y, z, c)),
    hops(lambda x, y, z, c: (x, y + 1, z, c)),
    hops(lambda x, y, z, c: (x, y - 1, z, c)),
)
TOKENS = (
    tile_hop(1, (0, 1)),
    tile_hop(1, (-1, 0)),
    tile_hop(-1, (0, 1)),
    tile_hop(-1, (-1, 0)),
    tile_hop(0, (-1, 1)),
)
ORDER = ((7, 11, 9, 1, 0, 3, 8, 6, 10, 2, 5, 4), (8, 11, 10, 2, 0, 4, 7, 6, 9, 1, 5, 3))

def send(x, pairs):
    return lax.ppermute(x, AXES, pairs)


def together(*values):
    return lax.optimization_barrier(values)


def cost(flops, nbytes, trans=0):
    return pl.CostEstimate(flops=int(flops), bytes_accessed=int(nbytes), transcendentals=int(trans))


def modulate_kernel(x_ref, scale_ref, shift_ref, o_ref):
    x = x_ref[...].astype(F32)
    mean = jnp.mean(x, axis=-1, keepdims=True)
    centred = x - mean
    var = jnp.mean(centred * centred, axis=-1, keepdims=True)
    normed = centred * lax.rsqrt(var + EPS)
    o_ref[...] = (normed * (1.0 + scale_ref[...]) + shift_ref[...]).astype(BF)


def modulate(x, scale, shift):
    rows, width = x.shape
    step = 64
    return pl.pallas_call(
        modulate_kernel,
        out_shape=jax.ShapeDtypeStruct((rows, width), BF),
        grid=(rows // step,),
        in_specs=[
            pl.BlockSpec((step, width), lambda i: (i, 0)),
            pl.BlockSpec((1, width), lambda i: (0, 0)),
            pl.BlockSpec((1, width), lambda i: (0, 0)),
        ],
        out_specs=pl.BlockSpec((step, width), lambda i: (i, 0)),
        cost_estimate=cost(rows * width * 8, rows * width * 4),
        name="modulate",
    )(x, scale.reshape(1, -1), shift.reshape(1, -1))


def head_norm(raw, gain):
    return (raw * lax.rsqrt(jnp.mean(raw * raw, axis=-1, keepdims=True) + EPS) * gain).astype(BF)


def heads_kernel(n, m, order_ref, far_ref, *refs):
    tiles, blocks = (refs[:n], refs[n : n + m])
    qg_ref, kg_ref, mine_ref, theirs_ref, buf, weight, q_ref, k_ref, v_ref, sem, wsem = refs[n + m :]
    i = pl.program_id(0)
    parts = wsem.shape[0]
    deep = weight.shape[0] // parts
    rows = buf.shape[1]
    steps = n

    def copies():
        for j in range(parts):
            each = parts // m
            block = blocks[j // each].at[pl.ds(j % each * deep, deep)]
            yield pltpu.make_async_copy(block, weight.at[pl.ds(j * deep, deep)], wsem.at[j])

    def fetch(j, _):
        for t in range(n):

            @pl.when(order_ref[j] == t)
            def _():
                pltpu.make_async_copy(tiles[t], buf.at[j], sem.at[j]).start()

        return 0

    @pl.when(i == 0)
    def _():
        for copy in copies():
            copy.start()
        lax.fori_loop(0, n, fetch, 0)
        for copy in copies():
            copy.wait()

    @pl.when(i < steps)
    def _():
        pltpu.make_async_copy(tiles[0], buf.at[i], sem.at[i]).wait()
        raw = jnp.dot(buf[i], weight[:, : 2 * HALF], preferred_element_type=F32)
        at = pl.ds(pl.multiple_of(i * rows, rows), rows)
        for h in range(3):
            k_ref[h, at] = head_norm(raw[:, h * HD : (h + 1) * HD], kg_ref[...])
            v_ref[h, at] = raw[:, HALF + h * HD : HALF + (h + 1) * HD].astype(BF)

    @pl.when(jnp.logical_or(i == 4, i == 7))
    def _():
        t = jnp.where(i == 4, 0, 1)
        raw = jnp.dot(buf[i], weight[:, 2 * HALF :], preferred_element_type=F32)
        for h in range(3):
            q_ref[t, h] = head_norm(raw[:, h * HD : (h + 1) * HD], qg_ref[...])

    @pl.when(i >= steps)
    def _():
        h, t = ((i - steps) // 2, lax.rem(i - steps, 2))
        q = q_ref[t, h]
        factor = 1.4426950408889634 / jnp.sqrt(F32(HD))
        scores, top = ([], None)
        for j in range(9):
            at = pl.multiple_of((t * 3 + j) * rows, rows)
            k = k_ref[h, pl.ds(at, rows), :]
            s = lax.dot_general(q, k, (((1,), (1,)), ((), ())), preferred_element_type=F32)
            scores.append(s)
            most = jnp.max(s, axis=-1, keepdims=True) - far_ref[t * 3 + j]
            top = most if top is None else jnp.maximum(top, most)
        total = jnp.zeros((rows, 1), F32)
        acc = jnp.zeros((rows, HD), F32)
        for j in range(9):
            at = pl.multiple_of((t * 3 + j) * rows, rows)
            v = v_ref[h, pl.ds(at, rows), :]
            expo = jnp.exp2((scores[j] - (top + far_ref[t * 3 + j])) * factor)
            total += jnp.sum(expo, axis=-1, keepdims=True)
            acc += jnp.dot(expo.astype(BF), v, preferred_element_type=F32)
        result = (acc / total).astype(BF)
        cols = pl.ds(pl.multiple_of(h * HD, HD), HD)

        @pl.when(t == 0)
        def _():
            mine_ref[:, cols] = result

        @pl.when(t == 1)
        def _():
            theirs_ref[:, cols] = result


def three_heads(order, far, tiles, blocks, q_gain, k_gain):
    n, m = (len(tiles), len(blocks))
    rows, width = tiles[0].shape
    hbm = pl.BlockSpec(memory_space=pltpu.HBM)
    return pl.pallas_call(
        functools.partial(heads_kernel, n, m),
        out_shape=[jax.ShapeDtypeStruct((rows, HALF), BF)] * 2,
        grid=(n + 6,),
        in_specs=[pl.BlockSpec(memory_space=pltpu.SMEM)] * 2
        + [hbm] * (n + m)
        + [pl.BlockSpec((1, HD), lambda i: (0, 0))] * 2,
        out_specs=[pl.BlockSpec((rows, HALF), lambda i: (0, 0))] * 2,
        scratch_shapes=[
            pltpu.VMEM((n, rows, width), BF),
            pltpu.VMEM((width, 3 * HALF), BF),
            pltpu.VMEM((2, 3, rows, HD), BF),
            pltpu.VMEM((3, n * rows, HD), BF),
            pltpu.VMEM((3, n * rows, HD), BF),
            pltpu.SemaphoreType.DMA((n,)),
            pltpu.SemaphoreType.DMA((4,)),
        ],
        compiler_params=pltpu.CompilerParams(vmem_limit_bytes=60 << 20),
        cost_estimate=cost(
            2 * (n * 2 + 2) * rows * width * HALF + 6 * rows * 9 * rows * HD * 4,
            (n * rows * width + width * 3 * HALF) * 2,
            6 * rows * 9 * rows,
        ),
        name="three_heads",
    )(order, far, *tiles, *blocks, q_gain, k_gain)


def project_kernel(c_ref, at_ref, a0, a1, a2, a3, w0, w1, gate_ref, o_ref, left):
    for j, a in enumerate((a0, a1, a2, a3)):
        left[:, pl.ds(pl.multiple_of(at_ref[j] * HALF, HD), HALF)] = a[...]
    for j, w in enumerate((w0, w1)):
        side = c_ref[0] if j == 0 else 1 - c_ref[0]
        cols = pl.ds(pl.multiple_of(side * 2 * HALF, HD), 2 * HALF)
        out = jnp.dot(left[...], w[...], preferred_element_type=F32)
        o_ref[:, cols] = (gate_ref[:, cols] * out).astype(BF)


def project_out(c, at, attended, pieces, gate):
    rows = attended[0].shape[0]
    width = pieces[0].shape[0]
    vmem = pl.BlockSpec(memory_space=pltpu.VMEM)
    return pl.pallas_call(
        project_kernel,
        out_shape=jax.ShapeDtypeStruct((rows, 4 * HALF), BF),
        in_specs=[pl.BlockSpec(memory_space=pltpu.SMEM)] * 2 + [vmem] * 7,
        out_specs=vmem,
        scratch_shapes=[pltpu.VMEM((rows, width), BF)],
        compiler_params=pltpu.CompilerParams(vmem_limit_bytes=16 << 20),
        cost_estimate=cost(2 * rows * width * 4 * HALF, width * 4 * HALF * 2 + rows * width * 4),
        name="project_out",
    )(c, at, *attended, *pieces, gate.reshape(1, -1))


def shards(tokens, shift, scale, gate, qkv_weight, out_weight, q_gain, k_gain):
    frames, tile_h, tile_w, width = tokens.shape
    count = frames * tile_h * tile_w
    x, l, z, u, c = (lax.axis_index(a) for a in AXES)
    parity = lax.rem(x + l, 2)
    h = x * 2 + l
    w = z * 2 + u

    def columns(core):
        at = (core * 2 + parity) * HALF
        parts = [lax.dynamic_slice_in_dim(qkv_weight, i * width + at, HALF, 1) for i in (1, 2, 0)]
        parts.append(lax.dynamic_slice_in_dim(out_weight, core * 2 * HALF, 2 * HALF, 1))
        return jnp.concatenate(parts, axis=1)

    mine, other = columns(c), send(columns(1 - c), SIBLING)
    pair = jnp.where(c == 0, jnp.concatenate([mine, other]), jnp.concatenate([other, mine]))
    other = send(pair, U_FLIP)
    flat, pair = together(tokens.reshape(count, width), pair)
    own = modulate(flat, scale, shift)
    own, other = together(own, other)
    quad = jnp.where(u == 0, jnp.concatenate([pair, other]), jnp.concatenate([other, pair]))
    w_in = lax.all_gather(quad[:, : 3 * HALF], "z", axis=0, tiled=True)
    w_out = lax.all_gather(quad[:, 3 * HALF :], "z", axis=0, tiled=True)
    quarter = width // 4
    w_in2 = [send(w_in[i * quarter : (i + 1) * quarter], pairs) for i, pairs in enumerate(NEAR)]

    arrived = [send(own, pairs) for pairs in TOKENS]
    tiles = [own] + arrived
    tiles += [send(t, SIBLING) for t in tiles]

    col_ok = [jnp.where(c == 0, w > 0, w < 15), True, True, jnp.where(c == 0, w < 15, w > 0)]
    row_ok = [h > 0, True, h < 7]
    far = jnp.stack([jnp.where(jnp.logical_and(a, b), 0.0, FAR).astype(F32) for a in col_ok for b in row_ok])
    order = jnp.where(c == 0, jnp.array(ORDER[0], jnp.int32), jnp.array(ORDER[1], jnp.int32))
    gains = (q_gain.reshape(1, HD), k_gain.reshape(1, HD))

    mine1, theirs1 = three_heads(order, far, tiles, [w_in], *gains)
    mine1, theirs1, *w_in2 = together(mine1, theirs1, *w_in2)
    mine3 = send(theirs1, SIBLING)
    mine2, theirs2 = three_heads(order, far, tiles, w_in2, *gains)
    mine2, theirs2, w_out = together(mine2, theirs2, w_out)
    mine4, w_out2 = send(theirs2, SIBLING), send(w_out, SIBLING)

    at = jnp.stack([c * 2 + parity, c * 2 + 1 - parity, (1 - c) * 2 + parity, (1 - c) * 2 + 1 - parity])
    attended = [mine1, mine2, mine3, mine4]
    out = project_out(c.reshape(1), at.astype(jnp.int32), attended, [w_out, w_out2], gate)
    return out.reshape(frames, tile_h, tile_w, width)


def solution(mesh):
    fine = Mesh(mesh.devices.reshape(SIZES), AXES)
    tile = P(None, ("x", "l"), ("z", "u", "c"), None)
    rows = P(("z", "u", "c"), None)
    return jax.shard_map(
        shards,
        mesh=fine,
        in_specs=(tile, P(), P(), P(), rows, rows, P(), P()),
        out_specs=tile,
        check_vma=False,
    )
```

```python
import functools
import itertools

import jax
import jax.numpy as jnp
from jax import lax
from jax.experimental import pallas as pl
from jax.experimental.pallas import tpu as pltpu
from jax.sharding import Mesh
from jax.sharding import PartitionSpec as P

HEADS = 12
HD = 128
TILE_T = 4
EPS = 1e-06
HALF = 3 * HD
AXES = ("x", "l", "z", "u", "c")
SIZES = (4, 2, 8, 2, 2)
FAR = 1e30
GROUP = 2
BF = jnp.bfloat16
F32 = jnp.float32


def hops(move):
    pairs = []
    for x, l, z, u, c in itertools.product(*map(range, SIZES)):
        x2, y2, z2, c2 = move(x, u * 2 + l, z, c)
        to = (x2 % 4, y2 % 2, z2 % 8, y2 % 4 // 2, c2)
        rank = [functools.reduce(lambda r, d: r * d[0] + d[1], zip(SIZES, at), 0) for at in ((x, l, z, u, c), to)]
        pairs.append(tuple(rank))
    return pairs


def tile_hop(down, across):
    def move(x, y, z, c):
        h, w = ((x * 2 + y % 2 + down) % 8, (z * 2 + y // 2 + across[c]) % 16)
        return h // 2, w % 2 * 2 + h % 2, w // 2, c

    return hops(move)


SIBLING = hops(lambda x, y, z, c: (x, y, z, 1 - c))
U_FLIP = hops(lambda x, y, z, c: (x, y + 2, z, c))
NEAR = (
    hops(lambda x, y, z, c: (x + 1, y, z, c)),
    hops(lambda x, y, z, c: (x - 1, y, z, c)),
    hops(lambda x, y, z, c: (x, y + 1, z, c)),
    hops(lambda x, y, z, c: (x, y - 1, z, c)),
)
TOKENS = (
    tile_hop(1, (0, 1)),
    tile_hop(1, (-1, 0)),
    tile_hop(-1, (0, 1)),
    tile_hop(-1, (-1, 0)),
    tile_hop(0, (-1, 1)),
)
ORDER = ((7, 11, 9, 1, 0, 3, 8, 6, 10, 2, 5, 4), (8, 11, 10, 2, 0, 4, 7, 6, 9, 1, 5, 3))

def send(x, pairs):
    return lax.ppermute(x, AXES, pairs)


def together(*values):
    return lax.optimization_barrier(values)


def cost(flops, nbytes, trans=0):
    return pl.CostEstimate(flops=int(flops), bytes_accessed=int(nbytes), transcendentals=int(trans))


def modulate_kernel(x_ref, scale_ref, shift_ref, o_ref):
    x = x_ref[...].astype(F32)
    mean = jnp.mean(x, axis=-1, keepdims=True)
    centred = x - mean
    var = jnp.mean(centred * centred, axis=-1, keepdims=True)
    normed = centred * lax.rsqrt(var + EPS)
    o_ref[...] = (normed * (1.0 + scale_ref[...]) + shift_ref[...]).astype(BF)


def modulate(x, scale, shift):
    rows, width = x.shape
    step = 64
    return pl.pallas_call(
        modulate_kernel,
        out_shape=jax.ShapeDtypeStruct((rows, width), BF),
        grid=(rows // step,),
        in_specs=[
            pl.BlockSpec((step, width), lambda i: (i, 0)),
            pl.BlockSpec((1, width), lambda i: (0, 0)),
            pl.BlockSpec((1, width), lambda i: (0, 0)),
        ],
        out_specs=pl.BlockSpec((step, width), lambda i: (i, 0)),
        cost_estimate=cost(rows * width * 8, rows * width * 4),
        name="modulate",
    )(x, scale.reshape(1, -1), shift.reshape(1, -1))


def head_norm(raw, gain):
    return (raw * lax.rsqrt(jnp.mean(raw * raw, axis=-1, keepdims=True) + EPS) * gain).astype(BF)


def heads_kernel(n, m, order_ref, far_ref, *refs):
    tiles, blocks = (refs[:n], refs[n : n + m])
    qg_ref, kg_ref, mine_ref, theirs_ref, buf, weight, q_ref, k_ref, v_ref, sem, wsem = refs[n + m :]
    i = pl.program_id(0)
    parts = wsem.shape[0]
    deep = weight.shape[0] // parts
    rows = buf.shape[0] // n
    steps = n // GROUP
    wide = GROUP * rows

    def copies():
        for j in range(parts):
            each = parts // m
            block = blocks[j // each].at[pl.ds(j % each * deep, deep)]
            yield pltpu.make_async_copy(block, weight.at[pl.ds(j * deep, deep)], wsem.at[j])

    def place(j):
        return buf.at[pl.ds(pl.multiple_of(j * rows, rows), rows)]

    def fetch(j, _):
        for t in range(n):

            @pl.when(order_ref[j] == t)
            def _():
                pltpu.make_async_copy(tiles[t], place(j), sem.at[j]).start()

        return 0

    @pl.when(i == 0)
    def _():
        for copy in copies():
            copy.start()
        lax.fori_loop(0, n, fetch, 0)
        for copy in copies():
            copy.wait()

    @pl.when(i < steps)
    def _():
        for j in range(GROUP):
            pltpu.make_async_copy(tiles[0], place(i * GROUP + j), sem.at[i * GROUP + j]).wait()
        for j in range(GROUP):
            at = pl.ds(pl.multiple_of(i * wide + j * rows, rows), rows)
            raw = jnp.dot(buf[at], weight[:, : 2 * HALF], preferred_element_type=F32)
            for h in range(3):
                k_ref[h, at] = head_norm(raw[:, h * HD : (h + 1) * HD], kg_ref[...])
                v_ref[h, at] = raw[:, HALF + h * HD : HALF + (h + 1) * HD].astype(BF)

    @pl.when(i == steps - 1)
    def _():
        for t, own in enumerate((4, 7)):
            x = buf[pl.ds(own * rows, rows)]
            raw = jnp.dot(x, weight[:, 2 * HALF :], preferred_element_type=F32)
            for h in range(3):
                q_ref[t, h] = head_norm(raw[:, h * HD : (h + 1) * HD], qg_ref[...])

    def attend(h, t):
        q = q_ref[t, h]
        factor = 1.4426950408889634 / jnp.sqrt(F32(HD))
        scores, top = ([], None)
        for j in range(9):
            k = k_ref[h, pl.ds((t * 3 + j) * rows, rows), :]
            s = lax.dot_general(q, k, (((1,), (1,)), ((), ())), preferred_element_type=F32)
            scores.append(s)
            most = jnp.max(s, axis=-1, keepdims=True) - far_ref[t * 3 + j]
            top = most if top is None else jnp.maximum(top, most)
        total = jnp.zeros((rows, 1), F32)
        acc = jnp.zeros((rows, HD), F32)
        for j in range(9):
            v = v_ref[h, pl.ds((t * 3 + j) * rows, rows), :]
            expo = jnp.exp2((scores[j] - (top + far_ref[t * 3 + j])) * factor)
            total += jnp.sum(expo, axis=-1, keepdims=True)
            acc += jnp.dot(expo.astype(BF), v, preferred_element_type=F32)
        return (acc / total).astype(BF)

    @pl.when(i >= steps)
    def _():
        h = i - steps
        cols = pl.ds(pl.multiple_of(h * HD, HD), HD)
        mine_ref[:, cols] = attend(h, 0)
        theirs_ref[:, cols] = attend(h, 1)


def three_heads(order, far, tiles, blocks, q_gain, k_gain):
    n, m = (len(tiles), len(blocks))
    rows, width = tiles[0].shape
    hbm = pl.BlockSpec(memory_space=pltpu.HBM)
    return pl.pallas_call(
        functools.partial(heads_kernel, n, m),
        out_shape=[jax.ShapeDtypeStruct((rows, HALF), BF)] * 2,
        grid=(n // GROUP + 3,),
        in_specs=[pl.BlockSpec(memory_space=pltpu.SMEM)] * 2
        + [hbm] * (n + m)
        + [pl.BlockSpec((1, HD), lambda i: (0, 0))] * 2,
        out_specs=[pl.BlockSpec((rows, HALF), lambda i: (0, 0))] * 2,
        scratch_shapes=[
            pltpu.VMEM((n * rows, width), BF),
            pltpu.VMEM((width, 3 * HALF), BF),
            pltpu.VMEM((2, 3, rows, HD), BF),
            pltpu.VMEM((3, n * rows, HD), BF),
            pltpu.VMEM((3, n * rows, HD), BF),
            pltpu.SemaphoreType.DMA((n,)),
            pltpu.SemaphoreType.DMA((4,)),
        ],
        compiler_params=pltpu.CompilerParams(vmem_limit_bytes=60 << 20),
        cost_estimate=cost(
            2 * (n * 2 + 2) * rows * width * HALF + 6 * rows * 9 * rows * HD * 4,
            (n * rows * width + width * 3 * HALF) * 2,
            6 * rows * 9 * rows,
        ),
        name="three_heads",
    )(order, far, *tiles, *blocks, q_gain, k_gain)


def project_kernel(c_ref, at_ref, a0, a1, a2, a3, w0, w1, gate_ref, o_ref, left, weight, asem, wsem):
    parts = wsem.shape[1]
    deep = weight.shape[1] // parts
    weights = [
        [pltpu.make_async_copy(w.at[rows], weight.at[i, rows], wsem.at[i, j]) for j, rows in enumerate(chunks)]
        for i, (w, chunks) in enumerate((w, [pl.ds(j * deep, deep) for j in range(parts)]) for w in (w0, w1))
    ]
    pieces = [
        pltpu.make_async_copy(a, left.at[:, pl.ds(pl.multiple_of(at_ref[j] * HALF, HD), HALF)], asem.at[j])
        for j, a in enumerate((a0, a1, a2, a3))
    ]
    for copy in pieces + weights[0] + weights[1]:
        copy.start()
    for copy in pieces:
        copy.wait()
    for side in range(2):
        for copy in weights[side]:
            copy.wait()
        core = c_ref[0] if side == 0 else 1 - c_ref[0]
        cols = pl.ds(pl.multiple_of(core * 2 * HALF, HD), 2 * HALF)
        out = jnp.dot(left[...], weight[side], preferred_element_type=F32)
        o_ref[:, cols] = (gate_ref[:, cols] * out).astype(BF)


def project_out(c, at, attended, halves, gate):
    rows = attended[0].shape[0]
    width = halves[0].shape[0]
    vmem = pl.BlockSpec(memory_space=pltpu.VMEM)
    smem = pl.BlockSpec(memory_space=pltpu.SMEM)
    held = pl.BlockSpec(memory_space=pl.ANY)
    return pl.pallas_call(
        project_kernel,
        out_shape=jax.ShapeDtypeStruct((rows, 4 * HALF), BF),
        in_specs=[smem] * 2 + [held] * 6 + [vmem],
        out_specs=vmem,
        scratch_shapes=[
            pltpu.VMEM((rows, width), BF),
            pltpu.VMEM((2, width, 2 * HALF), BF),
            pltpu.SemaphoreType.DMA((4,)),
            pltpu.SemaphoreType.DMA((2, 4)),
        ],
        compiler_params=pltpu.CompilerParams(vmem_limit_bytes=20 << 20),
        cost_estimate=cost(2 * rows * width * 4 * HALF, width * 4 * HALF * 2 + rows * width * 4),
        name="project_out",
    )(c, at, *attended, *halves, gate.reshape(1, -1))


def shards(tokens, shift, scale, gate, qkv_weight, out_weight, q_gain, k_gain):
    frames, tile_h, tile_w, width = tokens.shape
    count = frames * tile_h * tile_w
    x, l, z, u, c = (lax.axis_index(a) for a in AXES)
    parity = lax.rem(x + l, 2)
    h = x * 2 + l
    w = z * 2 + u

    def columns(core):
        at = (core * 2 + parity) * HALF
        parts = [lax.dynamic_slice_in_dim(qkv_weight, i * width + at, HALF, 1) for i in (1, 2, 0)]
        parts.append(lax.dynamic_slice_in_dim(out_weight, core * 2 * HALF, 2 * HALF, 1))
        return jnp.concatenate(parts, axis=1)

    mine, other = columns(c), send(columns(1 - c), SIBLING)
    pair = jnp.where(c == 0, jnp.concatenate([mine, other]), jnp.concatenate([other, mine]))
    other = send(pair, U_FLIP)
    flat, pair = together(tokens.reshape(count, width), pair)
    own = modulate(flat, scale, shift)
    own, other = together(own, other)
    quad = jnp.where(u == 0, jnp.concatenate([pair, other]), jnp.concatenate([other, pair]))
    w_in = lax.all_gather(quad[:, : 3 * HALF], "z", axis=0, tiled=True)
    w_out = lax.all_gather(quad[:, 3 * HALF :], "z", axis=0, tiled=True)
    quarter = width // 4
    w_in2 = [send(w_in[i * quarter : (i + 1) * quarter], pairs) for i, pairs in enumerate(NEAR)]

    arrived = [send(own, pairs) for pairs in TOKENS]
    tiles = [own] + arrived
    tiles += [send(t, SIBLING) for t in tiles]

    col_ok = [jnp.where(c == 0, w > 0, w < 15), True, True, jnp.where(c == 0, w < 15, w > 0)]
    row_ok = [h > 0, True, h < 7]
    far = jnp.stack([jnp.where(jnp.logical_and(a, b), 0.0, FAR).astype(F32) for a in col_ok for b in row_ok])
    order = jnp.where(c == 0, jnp.array(ORDER[0], jnp.int32), jnp.array(ORDER[1], jnp.int32))
    gains = (q_gain.reshape(1, HD), k_gain.reshape(1, HD))

    mine1, theirs1 = three_heads(order, far, tiles, [w_in], *gains)
    mine1, theirs1, *w_in2 = together(mine1, theirs1, *w_in2)
    mine3 = send(theirs1, SIBLING)
    mine2, theirs2 = three_heads(order, far, tiles, w_in2, *gains)
    mine2, theirs2, w_out = together(mine2, theirs2, w_out)
    mine4, w_out2 = send(theirs2, SIBLING), send(w_out, SIBLING)

    at = jnp.stack([c * 2 + parity, c * 2 + 1 - parity, (1 - c) * 2 + parity, (1 - c) * 2 + 1 - parity])
    attended = [mine1, mine2, mine3, mine4]
    out = project_out(c.reshape(1), at.astype(jnp.int32), attended, [w_out, w_out2], gate)
    return out.reshape(frames, tile_h, tile_w, width)


def solution(mesh):
    fine = Mesh(mesh.devices.reshape(SIZES), AXES)
    tile = P(None, ("x", "l"), ("z", "u", "c"), None)
    rows = P(("z", "u", "c"), None)
    return jax.shard_map(
        shards,
        mesh=fine,
        in_specs=(tile, P(), P(), P(), rows, rows, P(), P()),
        out_specs=tile,
        check_vma=False,
    )
```

```python
import functools
import itertools

import jax
import jax.numpy as jnp
from jax import lax
from jax.experimental import pallas as pl
from jax.experimental.pallas import tpu as pltpu
from jax.sharding import Mesh
from jax.sharding import PartitionSpec as P

HEADS = 12
HD = 128
TILE_T = 4
EPS = 1e-06
HALF = 3 * HD
AXES = ("x", "l", "z", "u", "c")
SIZES = (4, 2, 8, 2, 2)
FAR = 1e30
GROUP = 2
BF = jnp.bfloat16
F32 = jnp.float32


def hops(move):
    pairs = []
    for x, l, z, u, c in itertools.product(*map(range, SIZES)):
        x2, y2, z2, c2 = move(x, u * 2 + l, z, c)
        to = (x2 % 4, y2 % 2, z2 % 8, y2 % 4 // 2, c2)
        rank = [functools.reduce(lambda r, d: r * d[0] + d[1], zip(SIZES, at), 0) for at in ((x, l, z, u, c), to)]
        pairs.append(tuple(rank))
    return pairs


def tile_hop(down, across):
    def move(x, y, z, c):
        h, w = ((x * 2 + y % 2 + down) % 8, (z * 2 + y // 2 + across[c]) % 16)
        return h // 2, w % 2 * 2 + h % 2, w // 2, c

    return hops(move)


SIBLING = hops(lambda x, y, z, c: (x, y, z, 1 - c))
U_FLIP = hops(lambda x, y, z, c: (x, y + 2, z, c))
NEAR = (
    hops(lambda x, y, z, c: (x + 1, y, z, c)),
    hops(lambda x, y, z, c: (x - 1, y, z, c)),
    hops(lambda x, y, z, c: (x, y + 1, z, c)),
    hops(lambda x, y, z, c: (x, y - 1, z, c)),
)
TOKENS = (
    tile_hop(1, (0, 1)),
    tile_hop(1, (-1, 0)),
    tile_hop(-1, (0, 1)),
    tile_hop(-1, (-1, 0)),
    tile_hop(0, (-1, 1)),
)
ORDER = ((7, 11, 9, 1, 0, 3, 8, 6, 10, 2, 5, 4), (8, 11, 10, 2, 0, 4, 7, 6, 9, 1, 5, 3))

def send(x, pairs):
    return lax.ppermute(x, AXES, pairs)


def together(*values):
    return lax.optimization_barrier(values)


def cost(flops, nbytes, trans=0):
    return pl.CostEstimate(flops=int(flops), bytes_accessed=int(nbytes), transcendentals=int(trans))


def modulate_kernel(x_ref, scale_ref, shift_ref, o_ref):
    x = x_ref[...].astype(F32)
    mean = jnp.mean(x, axis=-1, keepdims=True)
    centred = x - mean
    var = jnp.mean(centred * centred, axis=-1, keepdims=True)
    normed = centred * lax.rsqrt(var + EPS)
    o_ref[...] = (normed * (1.0 + scale_ref[...]) + shift_ref[...]).astype(BF)


def modulate(x, scale, shift):
    rows, width = x.shape
    step = 64
    return pl.pallas_call(
        modulate_kernel,
        out_shape=jax.ShapeDtypeStruct((rows, width), BF),
        grid=(rows // step,),
        in_specs=[
            pl.BlockSpec((step, width), lambda i: (i, 0)),
            pl.BlockSpec((1, width), lambda i: (0, 0)),
            pl.BlockSpec((1, width), lambda i: (0, 0)),
        ],
        out_specs=pl.BlockSpec((step, width), lambda i: (i, 0)),
        cost_estimate=cost(rows * width * 8, rows * width * 4),
        name="modulate",
    )(x, scale.reshape(1, -1), shift.reshape(1, -1))


def head_norm(raw, gain):
    return (raw * lax.rsqrt(jnp.mean(raw * raw, axis=-1, keepdims=True) + EPS) * gain).astype(BF)


def heads_kernel(n, m, order_ref, far_ref, *refs):
    tiles, blocks = (refs[:n], refs[n : n + m])
    qg_ref, kg_ref, mine_ref, theirs_ref, buf, weight, q_ref, k_ref, v_ref, sem, wsem = refs[n + m :]
    i = pl.program_id(0)
    parts = wsem.shape[0]
    deep = weight.shape[0] // parts
    rows = buf.shape[0] // n
    steps = n // GROUP
    wide = GROUP * rows

    def copies():
        for j in range(parts):
            each = parts // m
            block = blocks[j // each].at[pl.ds(j % each * deep, deep)]
            yield pltpu.make_async_copy(block, weight.at[pl.ds(j * deep, deep)], wsem.at[j])

    def place(j):
        return buf.at[pl.ds(pl.multiple_of(j * rows, rows), rows)]

    def fetch(j, _):
        for t in range(n):

            @pl.when(order_ref[j] == t)
            def _():
                pltpu.make_async_copy(tiles[t], place(j), sem.at[j]).start()

        return 0

    @pl.when(i == 0)
    def _():
        for copy in copies():
            copy.start()
        lax.fori_loop(0, n, fetch, 0)
        for copy in copies():
            copy.wait()

    @pl.when(i < steps)
    def _():
        for j in range(GROUP):
            pltpu.make_async_copy(tiles[0], place(i * GROUP + j), sem.at[i * GROUP + j]).wait()
        for j in range(GROUP):
            at = pl.ds(pl.multiple_of(i * wide + j * rows, rows), rows)
            raw = jnp.dot(buf[at], weight[:, : 2 * HALF], preferred_element_type=F32)
            for h in range(3):
                k_ref[h, at] = head_norm(raw[:, h * HD : (h + 1) * HD], kg_ref[...])
                v_ref[h, at] = raw[:, HALF + h * HD : HALF + (h + 1) * HD].astype(BF)

    @pl.when(i == steps - 1)
    def _():
        for t, own in enumerate((4, 7)):
            x = buf[pl.ds(own * rows, rows)]
            raw = jnp.dot(x, weight[:, 2 * HALF :], preferred_element_type=F32)
            for h in range(3):
                q_ref[t, h] = head_norm(raw[:, h * HD : (h + 1) * HD], qg_ref[...])

    def attend(h, t):
        q = q_ref[t, h]
        factor = 1.4426950408889634 / jnp.sqrt(F32(HD))
        scores, top = ([], None)
        for j in range(9):
            k = k_ref[h, pl.ds((t * 3 + j) * rows, rows), :]
            s = lax.dot_general(q, k, (((1,), (1,)), ((), ())), preferred_element_type=F32)
            scores.append(s)
            most = jnp.max(s, axis=-1, keepdims=True) - far_ref[t * 3 + j]
            top = most if top is None else jnp.maximum(top, most)
        total = jnp.zeros((rows, 1), F32)
        acc = jnp.zeros((rows, HD), F32)
        for j in range(9):
            v = v_ref[h, pl.ds((t * 3 + j) * rows, rows), :]
            expo = jnp.exp2((scores[j] - (top + far_ref[t * 3 + j])) * factor)
            total += jnp.sum(expo, axis=-1, keepdims=True)
            acc += jnp.dot(expo.astype(BF), v, preferred_element_type=F32)
        return (acc / total).astype(BF)

    @pl.when(i >= steps)
    def _():
        h = i - steps
        cols = pl.ds(pl.multiple_of(h * HD, HD), HD)
        mine_ref[:, cols] = attend(h, 0)
        theirs_ref[:, cols] = attend(h, 1)


def three_heads(order, far, tiles, blocks, q_gain, k_gain):
    n, m = (len(tiles), len(blocks))
    rows, width = tiles[0].shape
    hbm = pl.BlockSpec(memory_space=pltpu.HBM)
    return pl.pallas_call(
        functools.partial(heads_kernel, n, m),
        out_shape=[jax.ShapeDtypeStruct((rows, HALF), BF)] * 2,
        grid=(n // GROUP + 3,),
        in_specs=[pl.BlockSpec(memory_space=pltpu.SMEM)] * 2
        + [hbm] * (n + m)
        + [pl.BlockSpec((1, HD), lambda i: (0, 0))] * 2,
        out_specs=[pl.BlockSpec((rows, HALF), lambda i: (0, 0))] * 2,
        scratch_shapes=[
            pltpu.VMEM((n * rows, width), BF),
            pltpu.VMEM((width, 3 * HALF), BF),
            pltpu.VMEM((2, 3, rows, HD), BF),
            pltpu.VMEM((3, n * rows, HD), BF),
            pltpu.VMEM((3, n * rows, HD), BF),
            pltpu.SemaphoreType.DMA((n,)),
            pltpu.SemaphoreType.DMA((4,)),
        ],
        compiler_params=pltpu.CompilerParams(vmem_limit_bytes=60 << 20),
        cost_estimate=cost(
            2 * (n * 2 + 2) * rows * width * HALF + 6 * rows * 9 * rows * HD * 4,
            (n * rows * width + width * 3 * HALF) * 2,
            6 * rows * 9 * rows,
        ),
        name="three_heads",
    )(order, far, *tiles, *blocks, q_gain, k_gain)


def columns_kernel(own, c_ref, at_ref, a0, a1, a2, a3, w_ref, gate_ref, *refs):
    before, (o_ref, left, weight, asem, wsem) = (refs[:-5], refs[-5:])
    parts = wsem.shape[0]
    deep = weight.shape[0] // parts
    copies = [
        pltpu.make_async_copy(a, left.at[:, pl.ds(pl.multiple_of(at_ref[j] * HALF, HD), HALF)], asem.at[j])
        for j, a in enumerate((a0, a1, a2, a3))
    ]
    for j in range(parts):
        rows = pl.ds(j * deep, deep)
        copies.append(pltpu.make_async_copy(w_ref.at[rows], weight.at[rows], wsem.at[j]))
    for copy in copies:
        copy.start()

    def span(core):
        return pl.ds(pl.multiple_of(core * 2 * HALF, HD), 2 * HALF)

    cols = span(c_ref[0] if own else 1 - c_ref[0])
    for copy in copies:
        copy.wait()
    out = jnp.dot(left[...], weight[...], preferred_element_type=F32)
    out = (gate_ref[:, cols] * out).astype(BF)
    if own:
        o_ref[...] = out
    else:
        o_ref[:, cols] = out
        o_ref[:, span(c_ref[0])] = before[0][...]


def out_columns(c, at, attended, w, gate, *before):
    own = not before
    rows = attended[0].shape[0]
    width = w.shape[0]
    vmem = pl.BlockSpec(memory_space=pltpu.VMEM)
    smem = pl.BlockSpec(memory_space=pltpu.SMEM)
    hbm = pl.BlockSpec(memory_space=pltpu.HBM)
    held = pl.BlockSpec(memory_space=pl.ANY)
    return pl.pallas_call(
        functools.partial(columns_kernel, own),
        out_shape=jax.ShapeDtypeStruct((rows, 2 * HALF if own else 4 * HALF), BF),
        in_specs=[smem] * 2 + [hbm] * 2 + [held] * 2 + [hbm if own else held] + [vmem] * (1 + len(before)),
        out_specs=vmem,
        scratch_shapes=[
            pltpu.VMEM((rows, width), BF),
            pltpu.VMEM((width, 2 * HALF), BF),
            pltpu.SemaphoreType.DMA((4,)),
            pltpu.SemaphoreType.DMA((4,)),
        ],
        compiler_params=pltpu.CompilerParams(vmem_limit_bytes=(60 if own else 20) << 20),
        cost_estimate=cost(2 * rows * width * 2 * HALF, width * 2 * HALF * 2 + rows * width * 3),
        name="out_columns",
    )(c, at, *attended, w, gate.reshape(1, -1), *before)


def shards(tokens, shift, scale, gate, qkv_weight, out_weight, q_gain, k_gain):
    frames, tile_h, tile_w, width = tokens.shape
    count = frames * tile_h * tile_w
    x, l, z, u, c = (lax.axis_index(a) for a in AXES)
    parity = lax.rem(x + l, 2)
    h = x * 2 + l
    w = z * 2 + u

    def columns(core):
        at = (core * 2 + parity) * HALF
        parts = [lax.dynamic_slice_in_dim(qkv_weight, i * width + at, HALF, 1) for i in (1, 2, 0)]
        parts.append(lax.dynamic_slice_in_dim(out_weight, core * 2 * HALF, 2 * HALF, 1))
        return jnp.concatenate(parts, axis=1)

    mine, other = columns(c), send(columns(1 - c), SIBLING)
    pair = jnp.where(c == 0, jnp.concatenate([mine, other]), jnp.concatenate([other, mine]))
    other = send(pair, U_FLIP)
    flat, pair = together(tokens.reshape(count, width), pair)
    own = modulate(flat, scale, shift)
    own, other = together(own, other)
    quad = jnp.where(u == 0, jnp.concatenate([pair, other]), jnp.concatenate([other, pair]))
    w_in = lax.all_gather(quad[:, : 3 * HALF], "z", axis=0, tiled=True)
    w_out = lax.all_gather(quad[:, 3 * HALF :], "z", axis=0, tiled=True)
    quarter = width // 4
    w_in2 = [send(w_in[i * quarter : (i + 1) * quarter], pairs) for i, pairs in enumerate(NEAR)]

    arrived = [send(own, pairs) for pairs in TOKENS]
    tiles = [own] + arrived
    tiles += [send(t, SIBLING) for t in tiles]

    col_ok = [jnp.where(c == 0, w > 0, w < 15), True, True, jnp.where(c == 0, w < 15, w > 0)]
    row_ok = [h > 0, True, h < 7]
    far = jnp.stack([jnp.where(jnp.logical_and(a, b), 0.0, FAR).astype(F32) for a in col_ok for b in row_ok])
    order = jnp.where(c == 0, jnp.array(ORDER[0], jnp.int32), jnp.array(ORDER[1], jnp.int32))
    gains = (q_gain.reshape(1, HD), k_gain.reshape(1, HD))

    mine1, theirs1 = three_heads(order, far, tiles, [w_in], *gains)
    mine1, theirs1, *w_in2 = together(mine1, theirs1, *w_in2)
    mine3 = send(theirs1, SIBLING)
    mine2, theirs2 = three_heads(order, far, tiles, w_in2, *gains)
    mine3, mine4, w_out = together(mine3, send(theirs2, SIBLING), w_out)
    w_out2 = send(w_out, SIBLING)

    at = jnp.stack([c * 2 + parity, c * 2 + 1 - parity, (1 - c) * 2 + parity, (1 - c) * 2 + 1 - parity])
    at, core = (at.astype(jnp.int32), c.reshape(1))
    attended = [mine1, mine2, mine3, mine4]
    columns_own = out_columns(core, at, attended, w_out, gate)
    columns_own, w_out2 = together(columns_own, w_out2)
    out = out_columns(core, at, attended, w_out2, gate, columns_own)
    return out.reshape(frames, tile_h, tile_w, width)


def solution(mesh):
    fine = Mesh(mesh.devices.reshape(SIZES), AXES)
    tile = P(None, ("x", "l"), ("z", "u", "c"), None)
    rows = P(("z", "u", "c"), None)
    return jax.shard_map(
        shards,
        mesh=fine,
        in_specs=(tile, P(), P(), P(), rows, rows, P(), P()),
        out_specs=tile,
        check_vma=False,
    )
```

```python
import functools
import itertools

import jax
import jax.numpy as jnp
from jax import lax
from jax.experimental import pallas as pl
from jax.experimental.pallas import tpu as pltpu
from jax.sharding import Mesh
from jax.sharding import PartitionSpec as P

HEADS = 12
HD = 128
TILE_T = 4
EPS = 1e-06
HALF = 3 * HD
AXES = ("x", "l", "z", "u", "c")
SIZES = (4, 2, 8, 2, 2)
FAR = 1e30
GROUP = 2
BF = jnp.bfloat16
F32 = jnp.float32


def hops(move):
    pairs = []
    for x, l, z, u, c in itertools.product(*map(range, SIZES)):
        x2, y2, z2, c2 = move(x, u * 2 + l, z, c)
        to = (x2 % 4, y2 % 2, z2 % 8, y2 % 4 // 2, c2)
        rank = [functools.reduce(lambda r, d: r * d[0] + d[1], zip(SIZES, at), 0) for at in ((x, l, z, u, c), to)]
        pairs.append(tuple(rank))
    return pairs


def tile_hop(down, across):
    def move(x, y, z, c):
        h, w = ((x * 2 + y % 2 + down) % 8, (z * 2 + y // 2 + across[c]) % 16)
        return h // 2, w % 2 * 2 + h % 2, w // 2, c

    return hops(move)


SIBLING = hops(lambda x, y, z, c: (x, y, z, 1 - c))
U_FLIP = hops(lambda x, y, z, c: (x, y + 2, z, c))
U_CROSS = hops(lambda x, y, z, c: (x, y + 2, z, 1 - c))
NEAR = (
    hops(lambda x, y, z, c: (x + 1, y, z, c)),
    hops(lambda x, y, z, c: (x - 1, y, z, c)),
    hops(lambda x, y, z, c: (x, y + 1, z, c)),
    hops(lambda x, y, z, c: (x, y - 1, z, c)),
)
TOKENS = (
    tile_hop(1, (0, 1)),
    tile_hop(1, (-1, 0)),
    tile_hop(-1, (0, 1)),
    tile_hop(-1, (-1, 0)),
    tile_hop(0, (-1, 1)),
)
ORDER = ((7, 11, 9, 1, 0, 3, 8, 6, 10, 2, 5, 4), (8, 11, 10, 2, 0, 4, 7, 6, 9, 1, 5, 3))

def send(x, pairs):
    return lax.ppermute(x, AXES, pairs)


def together(*values):
    return lax.optimization_barrier(values)


def cost(flops, nbytes, trans=0):
    return pl.CostEstimate(flops=int(flops), bytes_accessed=int(nbytes), transcendentals=int(trans))


def modulate_kernel(x_ref, scale_ref, shift_ref, o_ref):
    x = x_ref[...].astype(F32)
    mean = jnp.mean(x, axis=-1, keepdims=True)
    centred = x - mean
    var = jnp.mean(centred * centred, axis=-1, keepdims=True)
    normed = centred * lax.rsqrt(var + EPS)
    o_ref[...] = (normed * (1.0 + scale_ref[...]) + shift_ref[...]).astype(BF)


def modulate(x, scale, shift):
    rows, width = x.shape
    step = 64
    return pl.pallas_call(
        modulate_kernel,
        out_shape=jax.ShapeDtypeStruct((rows, width), BF),
        grid=(rows // step,),
        in_specs=[
            pl.BlockSpec((step, width), lambda i: (i, 0)),
            pl.BlockSpec((1, width), lambda i: (0, 0)),
            pl.BlockSpec((1, width), lambda i: (0, 0)),
        ],
        out_specs=pl.BlockSpec((step, width), lambda i: (i, 0)),
        cost_estimate=cost(rows * width * 8, rows * width * 4),
        name="modulate",
    )(x, scale.reshape(1, -1), shift.reshape(1, -1))


def head_norm(raw, gain):
    return (raw * lax.rsqrt(jnp.mean(raw * raw, axis=-1, keepdims=True) + EPS) * gain).astype(BF)


def heads_kernel(n, m, order_ref, far_ref, *refs):
    tiles, blocks = (refs[:n], refs[n : n + m])
    qg_ref, kg_ref, mine_ref, theirs_ref, buf, weight, q_ref, k_ref, v_ref, sem, wsem = refs[n + m :]
    i = pl.program_id(0)
    parts = wsem.shape[0]
    deep = weight.shape[0] // parts
    rows = buf.shape[0] // n
    steps = n // GROUP
    wide = GROUP * rows

    def copies():
        for j in range(parts):
            each = parts // m
            block = blocks[j // each].at[pl.ds(j % each * deep, deep)]
            yield pltpu.make_async_copy(block, weight.at[pl.ds(j * deep, deep)], wsem.at[j])

    def place(j):
        return buf.at[pl.ds(pl.multiple_of(j * rows, rows), rows)]

    def fetch(j, _):
        for t in range(n):

            @pl.when(order_ref[j] == t)
            def _():
                pltpu.make_async_copy(tiles[t], place(j), sem.at[j]).start()

        return 0

    @pl.when(i == 0)
    def _():
        for copy in copies():
            copy.start()
        lax.fori_loop(0, n, fetch, 0)
        for copy in copies():
            copy.wait()

    @pl.when(i < steps)
    def _():
        for j in range(GROUP):
            pltpu.make_async_copy(tiles[0], place(i * GROUP + j), sem.at[i * GROUP + j]).wait()
        for j in range(GROUP):
            at = pl.ds(pl.multiple_of(i * wide + j * rows, rows), rows)
            raw = jnp.dot(buf[at], weight[:, : 2 * HALF], preferred_element_type=F32)
            for h in range(3):
                k_ref[h, at] = head_norm(raw[:, h * HD : (h + 1) * HD], kg_ref[...])
                v_ref[h, at] = raw[:, HALF + h * HD : HALF + (h + 1) * HD].astype(BF)

    @pl.when(i == steps - 1)
    def _():
        for t, own in enumerate((4, 7)):
            x = buf[pl.ds(own * rows, rows)]
            raw = jnp.dot(x, weight[:, 2 * HALF :], preferred_element_type=F32)
            for h in range(3):
                q_ref[t, h] = head_norm(raw[:, h * HD : (h + 1) * HD], qg_ref[...])

    def attend(h, t):
        q = q_ref[t, h]
        factor = 1.4426950408889634 / jnp.sqrt(F32(HD))
        scores, top = ([], None)
        for j in range(9):
            k = k_ref[h, pl.ds((t * 3 + j) * rows, rows), :]
            s = lax.dot_general(q, k, (((1,), (1,)), ((), ())), preferred_element_type=F32)
            scores.append(s)
            most = jnp.max(s, axis=-1, keepdims=True) - far_ref[t * 3 + j]
            top = most if top is None else jnp.maximum(top, most)
        total = jnp.zeros((rows, 1), F32)
        acc = jnp.zeros((rows, HD), F32)
        for j in range(9):
            v = v_ref[h, pl.ds((t * 3 + j) * rows, rows), :]
            expo = jnp.exp2((scores[j] - (top + far_ref[t * 3 + j])) * factor)
            total += jnp.sum(expo, axis=-1, keepdims=True)
            acc += jnp.dot(expo.astype(BF), v, preferred_element_type=F32)
        return (acc / total).astype(BF)

    @pl.when(i >= steps)
    def _():
        h = i - steps
        cols = pl.ds(pl.multiple_of(h * HD, HD), HD)
        mine_ref[:, cols] = attend(h, 0)
        theirs_ref[:, cols] = attend(h, 1)


def three_heads(order, far, tiles, blocks, q_gain, k_gain):
    n, m = (len(tiles), len(blocks))
    rows, width = tiles[0].shape
    hbm = pl.BlockSpec(memory_space=pltpu.HBM)
    return pl.pallas_call(
        functools.partial(heads_kernel, n, m),
        out_shape=[jax.ShapeDtypeStruct((rows, HALF), BF)] * 2,
        grid=(n // GROUP + 3,),
        in_specs=[pl.BlockSpec(memory_space=pltpu.SMEM)] * 2
        + [hbm] * (n + m)
        + [pl.BlockSpec((1, HD), lambda i: (0, 0))] * 2,
        out_specs=[pl.BlockSpec((rows, HALF), lambda i: (0, 0))] * 2,
        scratch_shapes=[
            pltpu.VMEM((n * rows, width), BF),
            pltpu.VMEM((width, 3 * HALF), BF),
            pltpu.VMEM((2, 3, rows, HD), BF),
            pltpu.VMEM((3, n * rows, HD), BF),
            pltpu.VMEM((3, n * rows, HD), BF),
            pltpu.SemaphoreType.DMA((n,)),
            pltpu.SemaphoreType.DMA((4,)),
        ],
        compiler_params=pltpu.CompilerParams(vmem_limit_bytes=60 << 20),
        cost_estimate=cost(
            2 * (n * 2 + 2) * rows * width * HALF + 6 * rows * 9 * rows * HD * 4,
            (n * rows * width + width * 3 * HALF) * 2,
            6 * rows * 9 * rows,
        ),
        name="three_heads",
    )(order, far, *tiles, *blocks, q_gain, k_gain)


def columns_kernel(own, c_ref, at_ref, a0, a1, a2, a3, w_ref, gate_ref, *refs):
    before, (o_ref, left, weight, asem, wsem) = (refs[:-5], refs[-5:])
    parts = wsem.shape[0]
    deep = weight.shape[0] // parts
    copies = [
        pltpu.make_async_copy(a, left.at[:, pl.ds(pl.multiple_of(at_ref[j] * HALF, HD), HALF)], asem.at[j])
        for j, a in enumerate((a0, a1, a2, a3))
    ]
    for j in range(parts):
        rows = pl.ds(j * deep, deep)
        copies.append(pltpu.make_async_copy(w_ref.at[rows], weight.at[rows], wsem.at[j]))
    for copy in copies:
        copy.start()

    def span(core):
        return pl.ds(pl.multiple_of(core * 2 * HALF, HD), 2 * HALF)

    cols = span(c_ref[0] if own else 1 - c_ref[0])
    for copy in copies:
        copy.wait()
    out = jnp.dot(left[...], weight[...], preferred_element_type=F32)
    out = (gate_ref[:, cols] * out).astype(BF)
    if own:
        o_ref[...] = out
    else:
        o_ref[:, cols] = out
        o_ref[:, span(c_ref[0])] = before[0][...]


def out_columns(c, at, attended, w, gate, *before):
    own = not before
    rows = attended[0].shape[0]
    width = w.shape[0]
    vmem = pl.BlockSpec(memory_space=pltpu.VMEM)
    smem = pl.BlockSpec(memory_space=pltpu.SMEM)
    hbm = pl.BlockSpec(memory_space=pltpu.HBM)
    held = pl.BlockSpec(memory_space=pl.ANY)
    return pl.pallas_call(
        functools.partial(columns_kernel, own),
        out_shape=jax.ShapeDtypeStruct((rows, 2 * HALF if own else 4 * HALF), BF),
        in_specs=[smem] * 2 + [hbm] * 2 + [held] * 2 + [hbm if own else held] + [vmem] * (1 + len(before)),
        out_specs=vmem,
        scratch_shapes=[
            pltpu.VMEM((rows, width), BF),
            pltpu.VMEM((width, 2 * HALF), BF),
            pltpu.SemaphoreType.DMA((4,)),
            pltpu.SemaphoreType.DMA((4,)),
        ],
        compiler_params=pltpu.CompilerParams(vmem_limit_bytes=62 << 20),
        cost_estimate=cost(2 * rows * width * 2 * HALF, width * 2 * HALF * 2 + rows * width * 3),
        name="out_columns",
    )(c, at, *attended, w, gate.reshape(1, -1), *before)


def shards(tokens, shift, scale, gate, qkv_weight, out_weight, q_gain, k_gain):
    frames, tile_h, tile_w, width = tokens.shape
    count = frames * tile_h * tile_w
    x, l, z, u, c = (lax.axis_index(a) for a in AXES)
    parity = lax.rem(x + l, 2)
    h = x * 2 + l
    w = z * 2 + u

    def columns(core):
        at = (core * 2 + parity) * HALF
        parts = [lax.dynamic_slice_in_dim(qkv_weight, i * width + at, HALF, 1) for i in (1, 2, 0)]
        parts.append(lax.dynamic_slice_in_dim(out_weight, core * 2 * HALF, 2 * HALF, 1))
        return jnp.concatenate(parts, axis=1)

    mine, theirs = columns(c), columns(1 - c)
    sibling, same, cross = send(theirs, SIBLING), send(mine, U_FLIP), send(theirs, U_CROSS)
    flat, mine = together(tokens.reshape(count, width), mine)
    own = modulate(flat, scale, shift)
    own, sibling, same, cross = together(own, sibling, same, cross)

    def pair(first, second):
        return jnp.where(c == 0, jnp.concatenate([first, second]), jnp.concatenate([second, first]))

    near, away = pair(mine, sibling), pair(same, cross)
    quad = jnp.where(u == 0, jnp.concatenate([near, away]), jnp.concatenate([away, near]))
    w_in = lax.all_gather(quad[:, : 3 * HALF], "z", axis=0, tiled=True)
    w_out = lax.all_gather(quad[:, 3 * HALF :], "z", axis=0, tiled=True)
    quarter = width // 4
    w_in2 = [send(w_in[i * quarter : (i + 1) * quarter], pairs) for i, pairs in enumerate(NEAR)]

    arrived = [send(own, pairs) for pairs in TOKENS]
    tiles = [own] + arrived
    tiles += [send(t, SIBLING) for t in tiles]

    col_ok = [jnp.where(c == 0, w > 0, w < 15), True, True, jnp.where(c == 0, w < 15, w > 0)]
    row_ok = [h > 0, True, h < 7]
    far = jnp.stack([jnp.where(jnp.logical_and(a, b), 0.0, FAR).astype(F32) for a in col_ok for b in row_ok])
    order = jnp.where(c == 0, jnp.array(ORDER[0], jnp.int32), jnp.array(ORDER[1], jnp.int32))
    gains = (q_gain.reshape(1, HD), k_gain.reshape(1, HD))

    mine1, theirs1 = three_heads(order, far, tiles, [w_in], *gains)
    mine1, theirs1, *w_in2 = together(mine1, theirs1, *w_in2)
    mine3 = send(theirs1, SIBLING)
    mine2, theirs2 = three_heads(order, far, tiles, w_in2, *gains)
    mine3, mine4, w_out = together(mine3, send(theirs2, SIBLING), w_out)
    w_out2 = send(w_out, SIBLING)

    at = jnp.stack([c * 2 + parity, c * 2 + 1 - parity, (1 - c) * 2 + parity, (1 - c) * 2 + 1 - parity])
    at, core = (at.astype(jnp.int32), c.reshape(1))
    attended = [mine1, mine2, mine3, mine4]
    columns_own = out_columns(core, at, attended, w_out, gate)
    columns_own, w_out2 = together(columns_own, w_out2)
    out = out_columns(core, at, attended, w_out2, gate, columns_own)
    return out.reshape(frames, tile_h, tile_w, width)


def solution(mesh):
    fine = Mesh(mesh.devices.reshape(SIZES), AXES)
    tile = P(None, ("x", "l"), ("z", "u", "c"), None)
    rows = P(("z", "u", "c"), None)
    return jax.shard_map(
        shards,
        mesh=fine,
        in_specs=(tile, P(), P(), P(), rows, rows, P(), P()),
        out_specs=tile,
        check_vma=False,
    )
```

```python
import functools
import itertools

import jax
import jax.numpy as jnp
from jax import lax
from jax.experimental import pallas as pl
from jax.experimental.pallas import tpu as pltpu
from jax.sharding import Mesh
from jax.sharding import PartitionSpec as P

HEADS = 12
HD = 128
TILE_T = 4
EPS = 1e-06
HALF = 3 * HD
AXES = ("x", "l", "z", "u", "c")
SIZES = (4, 2, 8, 2, 2)
FAR = 1e30
GROUP = 4
BF = jnp.bfloat16
F32 = jnp.float32


def hops(move):
    pairs = []
    for x, l, z, u, c in itertools.product(*map(range, SIZES)):
        x2, y2, z2, c2 = move(x, u * 2 + l, z, c)
        to = (x2 % 4, y2 % 2, z2 % 8, y2 % 4 // 2, c2)
        rank = [functools.reduce(lambda r, d: r * d[0] + d[1], zip(SIZES, at), 0) for at in ((x, l, z, u, c), to)]
        pairs.append(tuple(rank))
    return pairs


def tile_hop(down, across):
    def move(x, y, z, c):
        h, w = ((x * 2 + y % 2 + down) % 8, (z * 2 + y // 2 + across[c]) % 16)
        return h // 2, w % 2 * 2 + h % 2, w // 2, c

    return hops(move)


SIBLING = hops(lambda x, y, z, c: (x, y, z, 1 - c))
U_FLIP = hops(lambda x, y, z, c: (x, y + 2, z, c))
U_CROSS = hops(lambda x, y, z, c: (x, y + 2, z, 1 - c))
NEAR = (
    hops(lambda x, y, z, c: (x + 1, y, z, c)),
    hops(lambda x, y, z, c: (x - 1, y, z, c)),
    hops(lambda x, y, z, c: (x, y + 1, z, c)),
    hops(lambda x, y, z, c: (x, y - 1, z, c)),
)
TOKENS = (
    tile_hop(1, (0, 1)),
    tile_hop(1, (-1, 0)),
    tile_hop(-1, (0, 1)),
    tile_hop(-1, (-1, 0)),
    tile_hop(0, (-1, 1)),
)
ORDER = ((7, 11, 9, 1, 0, 3, 8, 6, 10, 2, 5, 4), (8, 11, 10, 2, 0, 4, 7, 6, 9, 1, 5, 3))

def send(x, pairs):
    return lax.ppermute(x, AXES, pairs)


def together(*values):
    return lax.optimization_barrier(values)


def cost(flops, nbytes, trans=0):
    return pl.CostEstimate(flops=int(flops), bytes_accessed=int(nbytes), transcendentals=int(trans))


def modulate_kernel(x_ref, scale_ref, shift_ref, o_ref):
    x = x_ref[...].astype(F32)
    mean = jnp.mean(x, axis=-1, keepdims=True)
    centred = x - mean
    var = jnp.mean(centred * centred, axis=-1, keepdims=True)
    normed = centred * lax.rsqrt(var + EPS)
    o_ref[...] = (normed * (1.0 + scale_ref[...]) + shift_ref[...]).astype(BF)


def modulate(x, scale, shift):
    rows, width = x.shape
    step = 64
    return pl.pallas_call(
        modulate_kernel,
        out_shape=jax.ShapeDtypeStruct((rows, width), BF),
        grid=(rows // step,),
        in_specs=[
            pl.BlockSpec((step, width), lambda i: (i, 0)),
            pl.BlockSpec((1, width), lambda i: (0, 0)),
            pl.BlockSpec((1, width), lambda i: (0, 0)),
        ],
        out_specs=pl.BlockSpec((step, width), lambda i: (i, 0)),
        cost_estimate=cost(rows * width * 8, rows * width * 4),
        name="modulate",
    )(x, scale.reshape(1, -1), shift.reshape(1, -1))


def head_norm(raw, gain):
    return (raw * lax.rsqrt(jnp.mean(raw * raw, axis=-1, keepdims=True) + EPS) * gain).astype(BF)


def heads_kernel(n, m, order_ref, far_ref, *refs):
    tiles, blocks = (refs[:n], refs[n : n + m])
    qg_ref, kg_ref, mine_ref, theirs_ref, buf, weight, q_ref, k_ref, v_ref, sem, wsem = refs[n + m :]
    i = pl.program_id(0)
    parts = wsem.shape[0]
    deep = weight.shape[0] // parts
    rows = buf.shape[0] // n
    steps = n // GROUP
    wide = GROUP * rows

    def copies():
        for j in range(parts):
            each = parts // m
            block = blocks[j // each].at[pl.ds(j % each * deep, deep)]
            yield pltpu.make_async_copy(block, weight.at[pl.ds(j * deep, deep)], wsem.at[j])

    def place(j):
        return buf.at[pl.ds(pl.multiple_of(j * rows, rows), rows)]

    def fetch(j, _):
        for t in range(n):

            @pl.when(order_ref[j] == t)
            def _():
                pltpu.make_async_copy(tiles[t], place(j), sem.at[j]).start()

        return 0

    @pl.when(i == 0)
    def _():
        for copy in copies():
            copy.start()
        lax.fori_loop(0, n, fetch, 0)
        for copy in copies():
            copy.wait()

    @pl.when(i < steps)
    def _():
        for j in range(GROUP):
            pltpu.make_async_copy(tiles[0], place(i * GROUP + j), sem.at[i * GROUP + j]).wait()
        for j in range(GROUP):
            at = pl.ds(pl.multiple_of(i * wide + j * rows, rows), rows)
            raw = jnp.dot(buf[at], weight[:, : 2 * HALF], preferred_element_type=F32)
            for h in range(3):
                k_ref[h, at] = head_norm(raw[:, h * HD : (h + 1) * HD], kg_ref[...])
                v_ref[h, at] = raw[:, HALF + h * HD : HALF + (h + 1) * HD].astype(BF)

    @pl.when(i == steps - 1)
    def _():
        for t, own in enumerate((4, 7)):
            x = buf[pl.ds(own * rows, rows)]
            raw = jnp.dot(x, weight[:, 2 * HALF :], preferred_element_type=F32)
            for h in range(3):
                q_ref[t, h] = head_norm(raw[:, h * HD : (h + 1) * HD], qg_ref[...])

    def attend(h, t):
        q = q_ref[t, h]
        factor = 1.4426950408889634 / jnp.sqrt(F32(HD))
        scores, top = ([], None)
        for j in range(9):
            k = k_ref[h, pl.ds((t * 3 + j) * rows, rows), :]
            s = lax.dot_general(q, k, (((1,), (1,)), ((), ())), preferred_element_type=F32)
            scores.append(s)
            most = jnp.max(s, axis=-1, keepdims=True) - far_ref[t * 3 + j]
            top = most if top is None else jnp.maximum(top, most)
        total = jnp.zeros((rows, 1), F32)
        acc = jnp.zeros((rows, HD), F32)
        for j in range(9):
            v = v_ref[h, pl.ds((t * 3 + j) * rows, rows), :]
            expo = jnp.exp2((scores[j] - (top + far_ref[t * 3 + j])) * factor)
            total += jnp.sum(expo, axis=-1, keepdims=True)
            acc += jnp.dot(expo.astype(BF), v, preferred_element_type=F32)
        return (acc / total).astype(BF)

    @pl.when(i >= steps)
    def _():
        h = i - steps
        cols = pl.ds(pl.multiple_of(h * HD, HD), HD)
        mine_ref[:, cols] = attend(h, 0)
        theirs_ref[:, cols] = attend(h, 1)


def three_heads(order, far, tiles, blocks, q_gain, k_gain):
    n, m = (len(tiles), len(blocks))
    rows, width = tiles[0].shape
    hbm = pl.BlockSpec(memory_space=pltpu.HBM)
    return pl.pallas_call(
        functools.partial(heads_kernel, n, m),
        out_shape=[jax.ShapeDtypeStruct((rows, HALF), BF)] * 2,
        grid=(n // GROUP + 3,),
        in_specs=[pl.BlockSpec(memory_space=pltpu.SMEM)] * 2
        + [hbm] * (n + m)
        + [pl.BlockSpec((1, HD), lambda i: (0, 0))] * 2,
        out_specs=[pl.BlockSpec((rows, HALF), lambda i: (0, 0))] * 2,
        scratch_shapes=[
            pltpu.VMEM((n * rows, width), BF),
            pltpu.VMEM((width, 3 * HALF), BF),
            pltpu.VMEM((2, 3, rows, HD), BF),
            pltpu.VMEM((3, n * rows, HD), BF),
            pltpu.VMEM((3, n * rows, HD), BF),
            pltpu.SemaphoreType.DMA((n,)),
            pltpu.SemaphoreType.DMA((4,)),
        ],
        compiler_params=pltpu.CompilerParams(vmem_limit_bytes=60 << 20),
        cost_estimate=cost(
            2 * (n * 2 + 2) * rows * width * HALF + 6 * rows * 9 * rows * HD * 4,
            (n * rows * width + width * 3 * HALF) * 2,
            6 * rows * 9 * rows,
        ),
        name="three_heads",
    )(order, far, *tiles, *blocks, q_gain, k_gain)


def columns_kernel(own, c_ref, at_ref, a0, a1, a2, a3, w_ref, gate_ref, *refs):
    before, (o_ref, left, weight, asem, wsem) = (refs[:-5], refs[-5:])
    parts = wsem.shape[0]
    deep = weight.shape[0] // parts
    copies = [
        pltpu.make_async_copy(a, left.at[:, pl.ds(pl.multiple_of(at_ref[j] * HALF, HD), HALF)], asem.at[j])
        for j, a in enumerate((a0, a1, a2, a3))
    ]
    for j in range(parts):
        rows = pl.ds(j * deep, deep)
        copies.append(pltpu.make_async_copy(w_ref.at[rows], weight.at[rows], wsem.at[j]))
    for copy in copies:
        copy.start()

    def span(core):
        return pl.ds(pl.multiple_of(core * 2 * HALF, HD), 2 * HALF)

    cols = span(c_ref[0] if own else 1 - c_ref[0])
    for copy in copies[:4]:
        copy.wait()
    out = jnp.zeros(gate_ref[:, cols].shape, F32)
    for j in range(parts):
        copies[4 + j].wait()
        rows = pl.ds(j * deep, deep)
        out += jnp.dot(left[:, rows], weight[rows], preferred_element_type=F32)
    out = (gate_ref[:, cols] * out).astype(BF)
    if own:
        o_ref[...] = out
    else:
        o_ref[:, cols] = out
        o_ref[:, span(c_ref[0])] = before[0][...]


def out_columns(c, at, attended, w, gate, *before):
    own = not before
    rows = attended[0].shape[0]
    width = w.shape[0]
    vmem = pl.BlockSpec(memory_space=pltpu.VMEM)
    smem = pl.BlockSpec(memory_space=pltpu.SMEM)
    hbm = pl.BlockSpec(memory_space=pltpu.HBM)
    held = pl.BlockSpec(memory_space=pl.ANY)
    return pl.pallas_call(
        functools.partial(columns_kernel, own),
        out_shape=jax.ShapeDtypeStruct((rows, 2 * HALF if own else 4 * HALF), BF),
        in_specs=[smem] * 2 + [hbm] * 2 + [held] * 2 + [hbm if own else held] + [vmem] * (1 + len(before)),
        out_specs=vmem,
        scratch_shapes=[
            pltpu.VMEM((rows, width), BF),
            pltpu.VMEM((width, 2 * HALF), BF),
            pltpu.SemaphoreType.DMA((4,)),
            pltpu.SemaphoreType.DMA((4,)),
        ],
        compiler_params=pltpu.CompilerParams(vmem_limit_bytes=62 << 20),
        cost_estimate=cost(2 * rows * width * 2 * HALF, width * 2 * HALF * 2 + rows * width * 3),
        name="out_columns",
    )(c, at, *attended, w, gate.reshape(1, -1), *before)


def shards(tokens, shift, scale, gate, qkv_weight, out_weight, q_gain, k_gain):
    frames, tile_h, tile_w, width = tokens.shape
    count = frames * tile_h * tile_w
    x, l, z, u, c = (lax.axis_index(a) for a in AXES)
    parity = lax.rem(x + l, 2)
    h = x * 2 + l
    w = z * 2 + u

    def columns(core):
        at = (core * 2 + parity) * HALF
        parts = [lax.dynamic_slice_in_dim(qkv_weight, i * width + at, HALF, 1) for i in (1, 2, 0)]
        parts.append(lax.dynamic_slice_in_dim(out_weight, core * 2 * HALF, 2 * HALF, 1))
        return jnp.concatenate(parts, axis=1)

    mine, theirs = columns(c), columns(1 - c)
    sibling, same, cross = send(theirs, SIBLING), send(mine, U_FLIP), send(theirs, U_CROSS)
    flat, mine = together(tokens.reshape(count, width), mine)
    own = modulate(flat, scale, shift)
    own, sibling, same, cross = together(own, sibling, same, cross)

    def pair(first, second):
        return jnp.where(c == 0, jnp.concatenate([first, second]), jnp.concatenate([second, first]))

    near, away = pair(mine, sibling), pair(same, cross)
    quad = jnp.where(u == 0, jnp.concatenate([near, away]), jnp.concatenate([away, near]))
    w_in = lax.all_gather(quad[:, : 3 * HALF], "z", axis=0, tiled=True)
    w_out = lax.all_gather(quad[:, 3 * HALF :], "z", axis=0, tiled=True)
    quarter = width // 4
    w_in2 = [send(w_in[i * quarter : (i + 1) * quarter], pairs) for i, pairs in enumerate(NEAR)]

    arrived = [send(own, pairs) for pairs in TOKENS]
    tiles = [own] + arrived
    tiles += [send(t, SIBLING) for t in tiles]

    col_ok = [jnp.where(c == 0, w > 0, w < 15), True, True, jnp.where(c == 0, w < 15, w > 0)]
    row_ok = [h > 0, True, h < 7]
    far = jnp.stack([jnp.where(jnp.logical_and(a, b), 0.0, FAR).astype(F32) for a in col_ok for b in row_ok])
    order = jnp.where(c == 0, jnp.array(ORDER[0], jnp.int32), jnp.array(ORDER[1], jnp.int32))
    gains = (q_gain.reshape(1, HD), k_gain.reshape(1, HD))

    mine1, theirs1 = three_heads(order, far, tiles, [w_in], *gains)
    mine1, theirs1, *w_in2 = together(mine1, theirs1, *w_in2)
    mine3 = send(theirs1, SIBLING)
    mine2, theirs2 = three_heads(order, far, tiles, w_in2, *gains)
    mine3, mine4, w_out = together(mine3, send(theirs2, SIBLING), w_out)
    w_out2 = send(w_out, SIBLING)

    at = jnp.stack([c * 2 + parity, c * 2 + 1 - parity, (1 - c) * 2 + parity, (1 - c) * 2 + 1 - parity])
    at, core = (at.astype(jnp.int32), c.reshape(1))
    attended = [mine1, mine2, mine3, mine4]
    columns_own = out_columns(core, at, attended, w_out, gate)
    columns_own, w_out2 = together(columns_own, w_out2)
    out = out_columns(core, at, attended, w_out2, gate, columns_own)
    return out.reshape(frames, tile_h, tile_w, width)


def solution(mesh):
    fine = Mesh(mesh.devices.reshape(SIZES), AXES)
    tile = P(None, ("x", "l"), ("z", "u", "c"), None)
    rows = P(("z", "u", "c"), None)
    return jax.shard_map(
        shards,
        mesh=fine,
        in_specs=(tile, P(), P(), P(), rows, rows, P(), P()),
        out_specs=tile,
        check_vma=False,
    )
```
